256 devices in a mesh: chan: 32 (over x_lo, z, core), stn: 8 (over x_hi, y).
Axes of the slice: x: 4 (x_hi: 2, x_lo: 2; x = x_hi * 2 + x_lo), y: 4, z: 8, core: 2. Of those that a mesh axis runs over, the one named last changes fastest.
Arguments:
- voltages: bfloat16 [32, 2, 1024, 512], P(None, None, ('stn', 'chan')), may hold values from -6 to 6
- phase_index: int32 [1024], P(('stn', 'chan')), may hold values from 0 to 1023
- int_lengths: int32 [4], replicated, may hold values from 1 to 192, 512 in all
- beam_weights: bfloat16 [2, 256, 1024], replicated, may hold values from -0.1875 to 0.1875
Outputs:
- visibilities: bfloat16 [8, 5, 4, 32, 2, 128, 128], P('stn', None, None, 'chan')
- beam_power: float32 [4, 32, 256], P(None, 'chan', 'stn')
The draws below stay inside these ranges and needn't reach their ends.
Inputs may be any that keep to these rules, and one draw needn't show every extreme that they name: `int_lengths`: 4 integration lengths summing to 512; the longest is exactly 192.
All inputs are finite; a program needn't handle non-finite values.
Results may differ from the reference program's by a relative error of at most 0.0055.
Values may be sent and summed in bfloat16 or wider, within the bound.
A program may use at most 64 MiB of HBM per device.

```python
import math
import jax
import jax.numpy as jnp
import numpy as np
from jax import lax

SAMPLES = 512
INTEG = 4
MOST = 192
BLK = 128
BEAMS = 256
PHASES = 1024
CHANNELS = 32
INPUTS = 1024
PAIRS_DEV = 5
N_STN = 8


def touch_ends(values, stream_key, smallest, top_value):
    longest = values.shape.index(max(values.shape))
    spots = []
    for shift in (0, 1):
        where = [jax.random.randint(jax.random.fold_in(stream_key, axis), (), 0, length) for axis, length in enumerate(values.shape)]
        where[longest] = (where[longest] + shift) % values.shape[longest]
        spots.append(tuple(where))
    return values.at[spots[0]].set(smallest).at[spots[1]].set(top_value)


def block_scale(rng, extent, cuts, smallest, top_value):
    level = 1.0
    for dim, blocks in cuts:
        steps = jax.random.uniform(jax.random.fold_in(jax.random.fold_in(rng, 6), dim), (blocks,), jnp.float32, smallest / len(cuts), top_value / len(cuts))
        level = level * jnp.repeat(jnp.exp(steps), extent[dim] // blocks).reshape((-1,) + (1,) * (len(extent) - 1 - dim))
    return level


def length_profile(amount, total, limit, lean):
    weights = [(1 << 20) // math.isqrt(standing ** lean) + 1 for standing in range(2, amount + 1)]
    spare, holding = total - limit - (amount - 1), [1] * (amount - 1)
    while spare > 0:
        candidates = [i for i in range(amount - 1) if holding[i] < limit]
        whole, budget = sum([weights[i] for i in candidates]), spare
        for i in candidates:
            extra = min(limit - holding[i], max(1, budget * weights[i] // whole), spare)
            holding[i] = holding[i] + extra
            spare = spare - extra
    return np.array([limit] + holding)


def ragged(own_key, number_of, total, most, slope):
    if number_of == 2:
        one = jax.random.randint(own_key, (), max(1, total - most), min(most, total - 1) + 1)
        return jnp.stack([one, total - one])
    tallies = jnp.asarray(length_profile(number_of, total, most, slope), jnp.int32)
    pairs = (number_of - 1) // 2
    giver, receiver = tallies[1:1 + 2 * pairs:2], tallies[2:2 + 2 * pairs:2]
    margin = jnp.minimum(giver - 1, most - receiver)
    passed = jax.random.randint(jax.random.fold_in(own_key, 1), (pairs,), 0, 1 << 20) % (margin + 1)
    tallies = tallies.at[1:1 + 2 * pairs:2].set(giver - passed).at[2:2 + 2 * pairs:2].set(receiver + passed)
    return tallies[jax.random.permutation(jax.random.fold_in(own_key, 2), number_of)]


def bell_draw(own_key, extent, spread, reach, pieces=(), kind=jnp.bfloat16):
    entries = spread * jax.random.normal(own_key, extent, jnp.float32)
    if pieces:
        entries = entries * block_scale(own_key, extent, pieces, -0.22, 0.18)
    return jnp.clip(entries, -reach, reach).astype(kind)


def setup_inputs(seed: int = 0) -> dict:
    streams_of = jax.random.split(jax.random.key(seed), 5)
    voltages = bell_draw(streams_of[0], (CHANNELS, 2, INPUTS, SAMPLES), 1.0, 6.0, ((2, 256),))
    phase_index = touch_ends(jax.random.randint(streams_of[1], (INPUTS,), 0, PHASES), jax.random.fold_in(streams_of[1], 1), 0, PHASES - 1).astype(jnp.int32)
    int_lengths = ragged(streams_of[2], INTEG, SAMPLES, MOST, 0).astype(jnp.int32)
    beam_weights = bell_draw(streams_of[3], (2, BEAMS, INPUTS), INPUTS ** -0.5, 0.1875)
    return {"voltages": voltages, "phase_index": phase_index, "int_lengths": int_lengths, "beam_weights": beam_weights}


full_turn = 2.0 * math.pi


def rotate(voltages, phase_index, channel):
    phase_turns = (channel[:, None] * phase_index[None, :]) % PHASES
    phase_angle = phase_turns.astype(jnp.float32) * (full_turn / PHASES)
    cosine = jnp.cos(phase_angle)[:, :, None]
    sine_part = jnp.sin(phase_angle)[:, :, None]
    real_in = voltages[:, 0].astype(jnp.float32)
    imag_in = voltages[:, 1].astype(jnp.float32)
    return jnp.stack([real_in * cosine + imag_in * sine_part, imag_in * cosine - real_in * sine_part], axis=1).astype(jnp.bfloat16)


def windows(block, starts, int_lengths):
    padded = jnp.pad(block, ((0, 0), (0, 0), (0, MOST)))
    in_range = jnp.arange(MOST, dtype=jnp.int32)
    result = []
    for period in range(INTEG):
        segment = lax.dynamic_slice_in_dim(padded, starts[period], MOST, 2)
        keep_mask = (in_range < int_lengths[period])[None, None, :]
        result.append(jnp.where(keep_mask, segment, jnp.zeros_like(segment)))
    return jnp.stack(result)


def correlate(own_parts, other, starts, int_lengths):
    padded = jnp.pad(other, ((0, 0), (0, 0), (0, MOST)))
    block_rows = own_parts.shape[2] // 2
    result = []
    for period in range(INTEG):
        segment = lax.dynamic_slice_in_dim(padded, starts[period], MOST, 2)
        products = jnp.einsum('cal,cbl->cab', own_parts[period].astype(jnp.float32), segment.astype(jnp.float32), precision=lax.Precision.HIGHEST)
        real_part = products[:, :block_rows, :block_rows] + products[:, block_rows:, block_rows:]
        imag_part = products[:, block_rows:, :block_rows] - products[:, :block_rows, block_rows:]
        inverse = 1.0 / int_lengths[period].astype(jnp.float32)
        result.append((jnp.stack([real_part, imag_part], axis=1) * inverse).astype(jnp.bfloat16))
    return jnp.stack(result)


def stack_weights(beam_weights, columns):
    weight_real = beam_weights[0][:, columns]
    weight_imag = beam_weights[1][:, columns]
    upper = jnp.concatenate([weight_real, -weight_imag], axis=1)
    lower = jnp.concatenate([weight_imag, weight_real], axis=1)
    return jnp.concatenate([upper, lower], axis=0)


def reference(voltages, phase_index, int_lengths, beam_weights):
    channel = jnp.arange(CHANNELS, dtype=jnp.int32)
    rotated = rotate(voltages, phase_index, channel)
    starts = (jnp.cumsum(int_lengths) - int_lengths).astype(jnp.int32)
    blocks = [rotated[:, :, station * BLK:(station + 1) * BLK, :].reshape(CHANNELS, 2 * BLK, SAMPLES) for station in range(N_STN)]
    vis_rows = []
    for station in range(N_STN):
        own_parts = windows(blocks[station], starts, int_lengths)
        slots = []
        for offset in range(PAIRS_DEV):
            slots.append(correlate(own_parts, blocks[(station + offset) % N_STN], starts, int_lengths))
        vis_rows.append(jnp.stack(slots))
    visibilities = jnp.stack(vis_rows)
    beam_total = jnp.zeros((CHANNELS, 2 * BEAMS, SAMPLES), jnp.float32)
    for station in range(N_STN):
        stacked = stack_weights(beam_weights, slice(station * BLK, (station + 1) * BLK))
        partial_beam = jnp.einsum('rk,ckt->crt', stacked.astype(jnp.float32), blocks[station].astype(jnp.float32), precision=lax.Precision.HIGHEST)
        beam_total = beam_total + lax.optimization_barrier(partial_beam.astype(jnp.bfloat16)).astype(jnp.float32)
    beam_total = beam_total.reshape(CHANNELS, 2, BEAMS, SAMPLES)
    power = beam_total[:, 0] ** 2 + beam_total[:, 1] ** 2
    sample_index = jnp.arange(SAMPLES, dtype=jnp.int32)[None, :]
    in_window = ((sample_index >= starts[:, None]) & (sample_index < (starts + int_lengths)[:, None])).astype(jnp.float32)
    beam_power = jnp.einsum('cbt,jt->jcb', power, in_window, precision=lax.Precision.HIGHEST)
    beam_power = beam_power / int_lengths.astype(jnp.float32)[:, None, None]
    return visibilities, beam_power
```

```python
import functools
import math

import jax
import jax.numpy as jnp
from jax import lax
from jax.experimental import pallas as pl
from jax.experimental.pallas import tpu as pltpu
from jax.sharding import PartitionSpec as P

INTEG = 4
BEAMS = 256
PHASES = 1024
NC = 32
NS = 8
LT = 4
SAMPLES = 512
BLK = 128
OFFS = 5
SHARE = BEAMS // NS
NCH = 2
W = LT // NCH
BF = jnp.bfloat16
F32 = jnp.float32
MESH = pl.DeviceIdType.MESH


def rotate_all(ph, vin, sbuf, trig):
    row = lax.broadcasted_iota(jnp.int32, (NC, 8, 128), 1)
    chan = lax.broadcasted_iota(jnp.int32, (NC, 8, 128), 0)
    col = row % 4
    step = jnp.where(col == 0, ph[0], jnp.where(col == 1, ph[1], jnp.where(col == 2, ph[2], ph[3])))
    turns = chan * step - jnp.where(row >= 4, PHASES // 4, 0)
    turns = ((turns + PHASES // 2) & (PHASES - 1)) - PHASES // 2
    trig[...] = jnp.cos(turns.astype(F32) * (2.0 * math.pi / PHASES))

    def one(c, carry):
        cs = trig[c]
        cos, sin = cs[0:4], cs[4:8]
        re = vin[c, 0].astype(F32)
        im = vin[c, 1].astype(F32)
        for t in range(LT):
            a = re[:, t * 128 : (t + 1) * 128]
            b = im[:, t * 128 : (t + 1) * 128]
            sbuf[c, 0, t] = (a * cos + b * sin).astype(BF)
            sbuf[c, 1, t] = (b * cos - a * sin).astype(BF)
        return carry

    lax.fori_loop(0, NC, one, 0, unroll=4)


def comm_kernel(ph, v_hbm, g, vin, sbuf, trig, lsem, s1, r1, s2, r2):
    c = lax.axis_index("chan")
    s = lax.axis_index("stn")
    barrier = pltpu.get_barrier_semaphore()

    def hello(k, carry):
        pl.semaphore_signal(
            barrier, 1, device_id={"chan": (c + k) % NC, "stn": s}, device_id_type=MESH
        )
        return carry

    lax.fori_loop(1, NC, hello, 0)
    for k in range(1, NS):
        pl.semaphore_signal(
            barrier, 1, device_id={"chan": c, "stn": (s + k) % NS}, device_id_type=MESH
        )
    load = pltpu.make_async_copy(v_hbm, vin, lsem.at[0])
    load.start()
    load.wait()
    rotate_all(ph, vin, sbuf, trig)
    pl.semaphore_wait(barrier, NC - 1 + NS - 1)

    for q in range(NCH):
        ts = pl.ds(q * W, W)

        def send(k, carry):
            d = (c + k) % NC
            pltpu.make_async_remote_copy(
                sbuf.at[d, :, ts], g.at[0, :, ts, c], s1.at[q], r1.at[q],
                device_id={"chan": d, "stn": s}, device_id_type=MESH,
            ).start()
            return carry

        lax.fori_loop(1, NC, send, 0)
    for q in range(NCH):
        ts = pl.ds(q * W, W)
        own = pltpu.make_async_copy(sbuf.at[c, :, ts], g.at[0, :, ts, c], lsem.at[1])
        own.start()
        own.wait()
    sends = []
    for q in range(NCH):
        ts = pl.ds(q * W, W)
        many = pltpu.make_async_remote_copy(
            sbuf.at[pl.ds(0, NC - 1), :, ts], g.at[0, :, ts, pl.ds(0, NC - 1)], s1.at[q], r1.at[q],
            device_id={"chan": c, "stn": (s + 1) % NS}, device_id_type=MESH,
        )
        many.wait_recv()
        for k in range(1, NS):
            cp = pltpu.make_async_remote_copy(
                g.at[0, :, ts], g.at[k, :, ts], s2.at[k - 1, q], r2.at[k - 1, q],
                device_id={"chan": c, "stn": (s - k + NS) % NS}, device_id_type=MESH,
            )
            cp.start()
            sends.append(cp)
        many.wait_send()
    for cp in sends:
        cp.wait()


def comm(phase_index, voltages):
    return pl.pallas_call(
        comm_kernel,
        out_shape=jax.ShapeDtypeStruct((NS, 2, LT, NC, 4, 128), BF),
        in_specs=[pl.BlockSpec(memory_space=pltpu.SMEM), pl.BlockSpec(memory_space=pl.ANY)],
        out_specs=pl.BlockSpec(memory_space=pltpu.VMEM),
        scratch_shapes=[
            pltpu.VMEM((NC, 2, 4, SAMPLES), BF),
            pltpu.VMEM((NC, 2, LT, 4, 128), BF),
            pltpu.VMEM((NC, 8, 128), F32),
            pltpu.SemaphoreType.DMA((2,)),
            pltpu.SemaphoreType.DMA((NCH,)),
            pltpu.SemaphoreType.DMA((NCH,)),
            pltpu.SemaphoreType.DMA((NS - 1, NCH)),
            pltpu.SemaphoreType.DMA((NS - 1, NCH)),
        ],
        compiler_params=pltpu.CompilerParams(collective_id=0, has_side_effects=True),
        name="comm",
    )(phase_index, voltages)


def window_edges(lens):
    edges = [jnp.int32(0)]
    for j in range(INTEG):
        edges.append(edges[-1] + lens[j])
    return edges


def build_windows(blk, lens, left):
    edges = window_edges(lens)
    lane = lax.broadcasted_iota(jnp.int32, (1, 128), 1)
    for t in range(LT):
        at = lane + t * 128
        for j in range(INTEG):
            keep = ((at >= edges[j]) & (at < edges[j + 1])).astype(F32).astype(BF)
            for p in range(2):
                left[j * BLK : (j + 1) * BLK, (p * LT + t) * 128 : (p * LT + t + 1) * 128] = (
                    blk[p, t] * keep
                )


def correlate(blk, lens, left, put):
    re = [blk[0, t] for t in range(LT)]
    im = [blk[1, t] for t in range(LT)]
    neg = [-x for x in im]
    right = jnp.concatenate(
        [jnp.concatenate(re + im, axis=1), jnp.concatenate(neg + re, axis=1)], axis=0
    )
    prod = lax.dot_general(
        left[...], right, (((1,), (1,)), ((), ())), preferred_element_type=F32
    )
    for j in range(INTEG):
        inverse = 1.0 / jnp.full((1, 128), lens[j], jnp.int32).astype(F32)
        for p in range(2):
            put(j, p, (prod[j * BLK : (j + 1) * BLK, p * 128 : (p + 1) * 128] * inverse).astype(BF))


def beam_part(blk, wts, q):
    cols = pl.ds(pl.multiple_of(q * BLK, BLK), BLK)
    wr = wts[0, :, cols]
    wi = wts[1, :, cols]
    stack = jnp.concatenate(
        [jnp.concatenate([wr, -wi], axis=1), jnp.concatenate([wi, wr], axis=1)], axis=0
    )
    parts = []
    for t in range(0, LT, 2):
        x = jnp.concatenate(
            [jnp.concatenate([blk[p, t], blk[p, t + 1]], axis=1) for p in range(2)], axis=0
        )
        parts.append(jnp.dot(stack, x, preferred_element_type=F32))
    return jnp.concatenate(parts, axis=1)


def beam_finish(beam, lens, out):
    power = beam[:SHARE] ** 2 + beam[SHARE:] ** 2
    edges = window_edges(lens)
    at = lax.broadcasted_iota(jnp.int32, (8, SAMPLES), 1)
    row = lax.broadcasted_iota(jnp.int32, (8, SAMPLES), 0)
    mask = jnp.zeros((8, SAMPLES), F32)
    for j in range(INTEG):
        inside = (row == j) & (at >= edges[j]) & (at < edges[j + 1])
        mask = jnp.where(inside, 1.0, mask)
    total = lax.dot_general(
        mask, power, (((1,), (1,)), ((), ())), precision=lax.Precision.HIGHEST,
        preferred_element_type=F32,
    )
    for j in range(INTEG):
        out[j] = total[j : j + 1] / jnp.full((1, SHARE), lens[j], jnp.int32).astype(F32)


def math_kernel(lens, w_hbm, g_all, vis, power, wts, left, stage, wsem, osem):
    s = lax.axis_index("stn")
    load = pltpu.make_async_copy(
        w_hbm.at[:, pl.ds(pl.multiple_of(s * SHARE, SHARE), SHARE)], wts, wsem
    )
    load.start()
    g = g_all.reshape(NS, 2, LT, BLK, 128)
    build_windows(g.at[0], lens, left)
    for k in range(OFFS):

        def put(j, p, value):
            stage[k, j, p] = value

        correlate(g.at[k], lens, left, put)
        pltpu.make_async_copy(stage.at[k], vis.at[0, k, :, 0], osem.at[k]).start()
    load.wait()
    beam = jnp.zeros((2 * SHARE, SAMPLES), F32)
    for k in range(NS):
        beam = beam + beam_part(g.at[k], wts, (s + k) % NS)
    beam_finish(beam, lens, power)
    for k in range(OFFS):
        pltpu.make_async_copy(stage.at[k], vis.at[0, k, :, 0], osem.at[k]).wait()


def maths(int_lengths, beam_weights, gathered):
    return pl.pallas_call(
        math_kernel,
        out_shape=(
            jax.ShapeDtypeStruct((1, OFFS, INTEG, 1, 2, BLK, BLK), BF),
            jax.ShapeDtypeStruct((INTEG, 1, SHARE), F32),
        ),
        in_specs=[
            pl.BlockSpec(memory_space=pltpu.SMEM),
            pl.BlockSpec(memory_space=pl.ANY),
            pl.BlockSpec(memory_space=pltpu.VMEM),
        ],
        out_specs=(pl.BlockSpec(memory_space=pl.ANY), pl.BlockSpec(memory_space=pltpu.VMEM)),
        scratch_shapes=[
            pltpu.VMEM((2, SHARE, NS * BLK), BF),
            pltpu.VMEM((INTEG * BLK, 2 * SAMPLES), BF),
            pltpu.VMEM((OFFS, INTEG, 2, BLK, BLK), BF),
            pltpu.SemaphoreType.DMA,
            pltpu.SemaphoreType.DMA((OFFS,)),
        ],
        name="maths",
    )(int_lengths, beam_weights, gathered)


def local(voltages, phase_index, int_lengths, beam_weights):
    gathered = comm(phase_index, voltages)
    return maths(int_lengths, beam_weights, gathered)


def solution(mesh):
    return jax.shard_map(
        local,
        mesh=mesh,
        in_specs=(P(None, None, ("stn", "chan"), None), P(("stn", "chan")), P(), P()),
        out_specs=(P("stn", None, None, "chan", None, None, None), P(None, "chan", "stn")),
        check_vma=False,
    )
```

```python
import functools
import math

import jax
import jax.numpy as jnp
from jax import lax
from jax.experimental import pallas as pl
from jax.experimental.pallas import tpu as pltpu
from jax.sharding import PartitionSpec as P

INTEG = 4
BEAMS = 256
PHASES = 1024
NC = 32
NS = 8
LT = 4
SAMPLES = 512
BLK = 128
OFFS = 5
SHARE = BEAMS // NS
NCH = 4
W = LT // NCH
BF = jnp.bfloat16
F32 = jnp.float32
VMEM_LIMIT = 24 * 2**20
MESH = pl.DeviceIdType.MESH


def rotate_all(ph, vin, sbuf, trig):
    row = lax.broadcasted_iota(jnp.int32, (NC, 8, 128), 1)
    chan = lax.broadcasted_iota(jnp.int32, (NC, 8, 128), 0)
    col = row % 4
    step = jnp.where(col == 0, ph[0], jnp.where(col == 1, ph[1], jnp.where(col == 2, ph[2], ph[3])))
    turns = chan * step - jnp.where(row >= 4, PHASES // 4, 0)
    turns = ((turns + PHASES // 2) & (PHASES - 1)) - PHASES // 2
    trig[...] = jnp.cos(turns.astype(F32) * (2.0 * math.pi / PHASES))

    def one(c, carry):
        cs = trig[c]
        cos, sin = cs[0:4], cs[4:8]
        re = vin[c, 0].astype(F32)
        im = vin[c, 1].astype(F32)
        for t in range(LT):
            a = re[:, t * 128 : (t + 1) * 128]
            b = im[:, t * 128 : (t + 1) * 128]
            sbuf[c, 0, t] = (a * cos + b * sin).astype(BF)
            sbuf[c, 1, t] = (b * cos - a * sin).astype(BF)
        return carry

    lax.fori_loop(0, NC, one, 0, unroll=4)


def window_edges(lens):
    edges = [jnp.int32(0)]
    for j in range(INTEG):
        edges.append(edges[-1] + lens[j])
    return edges


def build_windows(blk, lens, left):
    edges = window_edges(lens)
    lane = lax.broadcasted_iota(jnp.int32, (1, 128), 1)
    for t in range(LT):
        at = lane + t * 128
        for j in range(INTEG):
            keep = ((at >= edges[j]) & (at < edges[j + 1])).astype(F32).astype(BF)
            for p in range(2):
                left[j * BLK : (j + 1) * BLK, (p * LT + t) * 128 : (p * LT + t + 1) * 128] = (
                    blk[p, t] * keep
                )


def correlate(blk, lens, left, put):
    re = [blk[0, t] for t in range(LT)]
    im = [blk[1, t] for t in range(LT)]
    neg = [-x for x in im]
    right = jnp.concatenate(
        [jnp.concatenate(re + im, axis=1), jnp.concatenate(neg + re, axis=1)], axis=0
    )
    prod = lax.dot_general(
        left[...], right, (((1,), (1,)), ((), ())), preferred_element_type=F32
    )
    for j in range(INTEG):
        inverse = 1.0 / jnp.full((1, 128), lens[j], jnp.int32).astype(F32)
        for p in range(2):
            put(j, p, (prod[j * BLK : (j + 1) * BLK, p * 128 : (p + 1) * 128] * inverse).astype(BF))


def beam_part(blk, wts, q):
    cols = pl.ds(pl.multiple_of(q * BLK, BLK), BLK)
    wr = wts[0, :, cols]
    wi = wts[1, :, cols]
    stack = jnp.concatenate(
        [jnp.concatenate([wr, -wi], axis=1), jnp.concatenate([wi, wr], axis=1)], axis=0
    )
    parts = []
    for t in range(0, LT, 2):
        x = jnp.concatenate(
            [jnp.concatenate([blk[p, t], blk[p, t + 1]], axis=1) for p in range(2)], axis=0
        )
        parts.append(jnp.dot(stack, x, preferred_element_type=F32))
    return jnp.concatenate(parts, axis=1)


def beam_finish(beam, lens, out):
    power = beam[:SHARE] ** 2 + beam[SHARE:] ** 2
    edges = window_edges(lens)
    at = lax.broadcasted_iota(jnp.int32, (8, SAMPLES), 1)
    row = lax.broadcasted_iota(jnp.int32, (8, SAMPLES), 0)
    mask = jnp.zeros((8, SAMPLES), F32)
    for j in range(INTEG):
        inside = (row == j) & (at >= edges[j]) & (at < edges[j + 1])
        mask = jnp.where(inside, 1.0, mask)
    total = lax.dot_general(
        mask, power, (((1,), (1,)), ((), ())), precision=lax.Precision.HIGHEST,
        preferred_element_type=F32,
    )
    for j in range(INTEG):
        out[j] = total[j : j + 1] / jnp.full((1, SHARE), lens[j], jnp.int32).astype(F32)


UP, DOWN, ACROSS = (0, 1), (0, -1), (1, 0)
FIRST = ((0, 4, ACROSS), (0, 1, UP), (0, 3, DOWN))


def second(q):
    if q % 2 == 0:
        return ((3, 7, ACROSS), (1, 2, UP), (4, 5, UP))
    return ((1, 5, ACROSS), (3, 2, DOWN), (4, 7, DOWN))


def third(q):
    return ((5, 6, UP), (7, 6, DOWN), (2, 6, ACROSS), (2, 6, ACROSS))[q]


def kernel(
    ph_hbm, lens_hbm, v_hbm, w_hbm, vis, power,
    ph, lens, g, vin, sbuf, trig, wts, left, stage, beam, lsem, s1, r1, s2, r2, osem,
):
    c = lax.axis_index("chan")
    s = lax.axis_index("stn")
    h, y = s // 4, s % 4

    def to(step):
        return {"chan": c, "stn": ((h + step[0]) % 2) * 4 + (y + step[1] + 4) % 4}

    barrier = pltpu.get_barrier_semaphore()

    def hello(k, carry):
        pl.semaphore_signal(
            barrier, 1, device_id={"chan": (c + k) % NC, "stn": s}, device_id_type=MESH
        )
        return carry

    lax.fori_loop(1, NC, hello, 0)
    for step in (UP, DOWN, ACROSS):
        pl.semaphore_signal(barrier, 1, device_id=to(step), device_id_type=MESH)
    load = pltpu.make_async_copy(v_hbm, vin, lsem.at[0])
    load.start()
    load_p = pltpu.make_async_copy(ph_hbm, ph, lsem.at[3])
    load_p.start()
    load_l = pltpu.make_async_copy(lens_hbm, lens, lsem.at[4])
    load_l.start()
    load_w = pltpu.make_async_copy(
        w_hbm.at[:, pl.ds(pl.multiple_of(s * SHARE, SHARE), SHARE)], wts, lsem.at[2]
    )
    load_w.start()
    load_p.wait()
    load.wait()
    rotate_all(ph, vin, sbuf, trig)
    pl.semaphore_wait(barrier, NC - 1 + 3)

    def span(q):
        return pl.ds(q * W, W)

    for q in range(NCH):

        def send(k, carry):
            d = (c + k) % NC
            pltpu.make_async_remote_copy(
                sbuf.at[d, :, span(q)], g.at[0, :, span(q), c], s1.at[q], r1.at[q],
                device_id={"chan": d, "stn": s}, device_id_type=MESH,
            ).start()
            return carry

        lax.fori_loop(1, NC, send, 0)
    own = pltpu.make_async_copy(sbuf.at[c], g.at[0, :, :, c], lsem.at[1])
    own.start()
    own.wait()
    load_w.wait()
    load_l.wait()

    sends = []
    have = {0: NCH}

    def copy(src, dst, q, step):
        return pltpu.make_async_remote_copy(
            g.at[src, :, span(q)], g.at[dst, :, span(q)], s2.at[dst, q], r2.at[dst, q],
            device_id=to(step), device_id_type=MESH,
        )

    def arrive(slot, upto):
        while have.get(slot, 0) < upto:
            q = have.get(slot, 0)
            copy(0, slot, q, UP).wait_recv()
            have[slot] = q + 1

    def push(src, dst, step, q):
        arrive(src, q + 1)
        cp = copy(src, dst, q, step)
        cp.start()
        sends.append(cp)

    blocks = g.reshape(NS, 2, LT, BLK, 128)

    def process(slot):
        arrive(slot, NCH)
        dh, dy = slot // 4, slot % 4
        q = ((h + dh) % 2) * 4 + (y - dy + 4) % 4
        k = (q - s + NS) % NS
        part = beam_part(blocks.at[slot], wts, q)
        beam[...] = part if slot == 0 else beam[...] + part

        def vis_block():
            def put(j, p, value):
                stage[k, j, p] = value

            correlate(blocks.at[slot], lens, left, put)
            pltpu.make_async_copy(stage.at[k], vis.at[0, k, :, 0], osem.at[k]).start()

        if slot == 0:
            vis_block()
        else:
            pl.when(k < OFFS)(vis_block)

    for q in range(NCH):
        turned = pltpu.make_async_remote_copy(
            sbuf.at[pl.ds(0, NC - 1), :, span(q)], g.at[0, :, span(q), pl.ds(0, NC - 1)],
            s1.at[q], r1.at[q], device_id=to(UP), device_id_type=MESH,
        )
        turned.wait_recv()
        for src, dst, step in FIRST:
            push(src, dst, step, q)
        turned.wait_send()
    build_windows(blocks.at[0], lens, left)
    process(0)
    for q in range(NCH):
        for src, dst, step in second(q):
            push(src, dst, step, q)
    for slot in (4, 1, 3):
        process(slot)
    for q in range(NCH):
        push(*third(q), q)
    for slot in (2, 5, 7, 6):
        process(slot)
    beam_finish(beam[...], lens, power)
    for cp in sends:
        cp.wait_send()
    for k in range(OFFS):
        pltpu.make_async_copy(stage.at[k], vis.at[0, k, :, 0], osem.at[k]).wait()


def local(voltages, phase_index, int_lengths, beam_weights):
    return pl.pallas_call(
        kernel,
        out_shape=(
            jax.ShapeDtypeStruct((1, OFFS, INTEG, 1, 2, BLK, BLK), BF),
            jax.ShapeDtypeStruct((INTEG, 1, SHARE), F32),
        ),
        in_specs=[
            pl.BlockSpec(memory_space=pltpu.HBM),
            pl.BlockSpec(memory_space=pltpu.HBM),
            pl.BlockSpec(memory_space=pltpu.HBM),
            pl.BlockSpec(memory_space=pltpu.HBM),
        ],
        out_specs=(pl.BlockSpec(memory_space=pl.ANY), pl.BlockSpec(memory_space=pltpu.VMEM)),
        scratch_shapes=[
            pltpu.SMEM((INTEG,), jnp.int32),
            pltpu.SMEM((INTEG,), jnp.int32),
            pltpu.VMEM((NS, 2, LT, NC, 4, 128), BF),
            pltpu.VMEM((NC, 2, 4, SAMPLES), BF),
            pltpu.VMEM((NC, 2, LT, 4, 128), BF),
            pltpu.VMEM((NC, 8, 128), F32),
            pltpu.VMEM((2, SHARE, NS * BLK), BF),
            pltpu.VMEM((INTEG * BLK, 2 * SAMPLES), BF),
            pltpu.VMEM((OFFS, INTEG, 2, BLK, BLK), BF),
            pltpu.VMEM((2 * SHARE, SAMPLES), F32),
            pltpu.SemaphoreType.DMA((5,)),
            pltpu.SemaphoreType.DMA((NCH,)),
            pltpu.SemaphoreType.DMA((NCH,)),
            pltpu.SemaphoreType.DMA((NS, NCH)),
            pltpu.SemaphoreType.DMA((NS, NCH)),
            pltpu.SemaphoreType.DMA((OFFS,)),
        ],
        compiler_params=pltpu.CompilerParams(
            collective_id=0, has_side_effects=True, vmem_limit_bytes=VMEM_LIMIT
        ),
        name="correlator",
    )(
        *[
            pltpu.with_memory_space_constraint(x, pltpu.HBM)
            for x in (phase_index, int_lengths, voltages, beam_weights)
        ]
    )


def solution(mesh):
    return jax.shard_map(
        local,
        mesh=mesh,
        in_specs=(P(None, None, ("stn", "chan"), None), P(("stn", "chan")), P(), P()),
        out_specs=(P("stn", None, None, "chan", None, None, None), P(None, "chan", "stn")),
        check_vma=False,
    )
```

```python
import functools
import math

import jax
import jax.numpy as jnp
from jax import lax
from jax.experimental import pallas as pl
from jax.experimental.pallas import tpu as pltpu
from jax.sharding import PartitionSpec as P

INTEG = 4
BEAMS = 256
PHASES = 1024
NC = 32
NS = 8
LT = 4
SAMPLES = 512
BLK = 128
OFFS = 5
SHARE = BEAMS // NS
NCH = LT
BF = jnp.bfloat16
FAR = sorted(range(1, NC), key=lambda k: -min(k % 16, 16 - k % 16))
F32 = jnp.float32
VMEM_LIMIT = 24 * 2**20
MESH = pl.DeviceIdType.MESH


def rotate_all(ph, vin, sbuf, trig):
    row = lax.broadcasted_iota(jnp.int32, (NC, 8, 128), 1)
    chan = lax.broadcasted_iota(jnp.int32, (NC, 8, 128), 0)
    col = row % 4
    step = jnp.where(col == 0, ph[0], jnp.where(col == 1, ph[1], jnp.where(col == 2, ph[2], ph[3])))
    turns = chan * step - jnp.where(row >= 4, PHASES // 4, 0)
    turns = ((turns + PHASES // 2) & (PHASES - 1)) - PHASES // 2
    trig[...] = jnp.cos(turns.astype(F32) * (2.0 * math.pi / PHASES))

    def one(c, carry):
        cs = trig[c]
        cos, sin = cs[0:4], cs[4:8]
        re = vin[c, 0].astype(F32)
        im = vin[c, 1].astype(F32)
        for t in range(LT):
            a = re[:, t * 128 : (t + 1) * 128]
            b = im[:, t * 128 : (t + 1) * 128]
            sbuf[t, c, 0] = (a * cos + b * sin).astype(BF)
            sbuf[t, c, 1] = (b * cos - a * sin).astype(BF)
        return carry

    lax.fori_loop(0, NC, one, 0, unroll=4)


def window_edges(lens):
    edges = [jnp.int32(0)]
    for j in range(INTEG):
        edges.append(edges[-1] + lens[j])
    return edges


def build_windows(blk, lens, left):
    edges = window_edges(lens)
    lane = lax.broadcasted_iota(jnp.int32, (1, 128), 1)
    for t in range(LT):
        at = lane + t * 128
        for j in range(INTEG):
            keep = ((at >= edges[j]) & (at < edges[j + 1])).astype(F32).astype(BF)
            for p in range(2):
                left[j * BLK : (j + 1) * BLK, (p * LT + t) * 128 : (p * LT + t + 1) * 128] = (
                    blk[p, t] * keep
                )


def products(blk, left, lo, hi):
    re = [blk[0, t] for t in range(lo, hi)]
    im = [blk[1, t] for t in range(lo, hi)]
    neg = [-x for x in im]
    right = jnp.concatenate(
        [jnp.concatenate(re + im, axis=1), jnp.concatenate(neg + re, axis=1)], axis=0
    )
    if (lo, hi) == (0, LT):
        rows = left[...]
    else:
        rows = jnp.concatenate(
            [left[:, (p * LT + lo) * 128 : (p * LT + hi) * 128] for p in range(2)], axis=1
        )
    return lax.dot_general(rows, right, (((1,), (1,)), ((), ())), preferred_element_type=F32)


def average(prod, lens, put):
    for j in range(INTEG):
        inverse = 1.0 / jnp.full((1, 128), lens[j], jnp.int32).astype(F32)
        for p in range(2):
            put(j, p, (prod[j * BLK : (j + 1) * BLK, p * 128 : (p + 1) * 128] * inverse).astype(BF))


def beam_part(blk, wts, q, lo, hi):
    cols = pl.ds(pl.multiple_of(q * BLK, BLK), BLK)
    wr = wts[0, :, cols]
    wi = wts[1, :, cols]
    stack = jnp.concatenate(
        [jnp.concatenate([wr, -wi], axis=1), jnp.concatenate([wi, wr], axis=1)], axis=0
    )
    parts = []
    for t in range(lo, hi, 2):
        x = jnp.concatenate(
            [jnp.concatenate([blk[p, u] for u in range(t, min(t + 2, hi))], axis=1) for p in range(2)],
            axis=0,
        )
        parts.append(jnp.dot(stack, x, preferred_element_type=F32))
    return jnp.concatenate(parts, axis=1)


def window_powers(beam, lens, lo):
    power = beam[:SHARE] ** 2 + beam[SHARE:] ** 2
    width = beam.shape[1]
    edges = window_edges(lens)
    at = lax.broadcasted_iota(jnp.int32, (8, width), 1) + lo * 128
    row = lax.broadcasted_iota(jnp.int32, (8, width), 0)
    mask = jnp.zeros((8, width), F32)
    for j in range(INTEG):
        inside = (row == j) & (at >= edges[j]) & (at < edges[j + 1])
        mask = jnp.where(inside, 1.0, mask)
    return lax.dot_general(
        mask, power, (((1,), (1,)), ((), ())), precision=lax.Precision.HIGHEST,
        preferred_element_type=F32,
    )


UP, DOWN, ACROSS = (0, 1), (0, -1), (1, 0)
FIRST = ((0, 4, ACROSS), (0, 1, UP), (0, 3, DOWN))


def second(q):
    if q % 2 == 0:
        return ((3, 7, ACROSS), (1, 2, UP), (4, 5, UP))
    return ((1, 5, ACROSS), (3, 2, DOWN), (4, 7, DOWN))


def third(q):
    return ((5, 6, UP), (7, 6, DOWN), (2, 6, ACROSS), (2, 6, ACROSS))[q]


def kernel(
    ph_hbm, lens_hbm, v_hbm, w_hbm, vis, power,
    ph, lens, g, vin, sbuf, trig, wts, left, beam, acc, sums, lsem, o1, s1, r1, s2, r2,
):
    c = lax.axis_index("chan")
    s = lax.axis_index("stn")
    h, y = s // 4, s % 4

    def to(step):
        return {"chan": c, "stn": ((h + step[0]) % 2) * 4 + (y + step[1] + 4) % 4}

    barrier = pltpu.get_barrier_semaphore()

    for k in FAR:
        pl.semaphore_signal(
            barrier, 1, device_id={"chan": (c + k) % NC, "stn": s}, device_id_type=MESH
        )
    for step in (UP, DOWN, ACROSS):
        pl.semaphore_signal(barrier, 1, device_id=to(step), device_id_type=MESH)
    load = pltpu.make_async_copy(v_hbm, vin, lsem.at[0])
    load.start()
    load_p = pltpu.make_async_copy(ph_hbm, ph, lsem.at[3])
    load_p.start()
    load_l = pltpu.make_async_copy(lens_hbm, lens, lsem.at[4])
    load_l.start()
    load_w = pltpu.make_async_copy(
        w_hbm.at[:, pl.ds(pl.multiple_of(s * SHARE, SHARE), SHARE)], wts, lsem.at[2]
    )
    load_w.start()
    load_p.wait()
    load.wait()
    rotate_all(ph, vin, sbuf, trig)
    pl.semaphore_wait(barrier, NC - 1 + 3)

    for q in range(NCH):
        for k in FAR:
            d = (c + k) % NC
            pltpu.make_async_remote_copy(
                sbuf.at[q, d], g.at[0, :, q, c], s1.at[q], r1.at[q],
                device_id={"chan": d, "stn": s}, device_id_type=MESH,
            ).start()
    owns = [
        pltpu.make_async_copy(sbuf.at[q, c], g.at[0, :, q, c], o1.at[q]) for q in range(NCH)
    ]
    for cp in owns:
        cp.start()
    for cp in owns:
        cp.wait()
    load_w.wait()
    load_l.wait()

    sends = []
    have = {0: NCH}

    def copy(src, dst, q, step):
        return pltpu.make_async_remote_copy(
            g.at[src, :, q], g.at[dst, :, q], s2.at[dst, q], r2.at[dst, q],
            device_id=to(step), device_id_type=MESH,
        )

    def arrive(slot, upto):
        while have.get(slot, 0) < upto:
            q = have.get(slot, 0)
            copy(0, slot, q, UP).wait_recv()
            have[slot] = q + 1

    def push(src, dst, step, q):
        arrive(src, q + 1)
        cp = copy(src, dst, q, step)
        cp.start()
        sends.append(cp)

    blocks = g.reshape(NS, 2, LT, BLK, 128)

    def block_at(slot):
        dh, dy = slot // 4, slot % 4
        q = ((h + dh) % 2) * 4 + (y - dy + 4) % 4
        return q, (q - s + NS) % NS

    def process(slot):
        arrive(slot, NCH)
        q, k = block_at(slot)
        part = beam_part(blocks.at[slot], wts, q, 0, LT)
        beam[...] = part if slot == 0 else beam[...] + part

        def vis_block():
            def put(j, p, value):
                vis[0, k, j, 0, p] = value

            average(products(blocks.at[slot], left, 0, LT), lens, put)

        if slot == 0:
            vis_block()
        else:
            pl.when(k < OFFS)(vis_block)

    def process_last(slot, cut):
        q, k = block_at(slot)
        arrive(slot, cut)

        @pl.when(k < OFFS)
        def _():
            acc[...] = products(blocks.at[slot], left, 0, cut)

        head = beam[:, : cut * 128] + beam_part(blocks.at[slot], wts, q, 0, cut)
        sums[...] = window_powers(head, lens, 0)
        arrive(slot, NCH)
        rest = beam[:, cut * 128 :] + beam_part(blocks.at[slot], wts, q, cut, LT)
        total = sums[...] + window_powers(rest, lens, cut)
        for j in range(INTEG):
            power[j] = total[j : j + 1] / jnp.full((1, SHARE), lens[j], jnp.int32).astype(F32)

        @pl.when(k < OFFS)
        def _():
            def put(j, p, value):
                vis[0, k, j, 0, p] = value

            average(acc[...] + products(blocks.at[slot], left, cut, LT), lens, put)

    for q in range(NCH):
        turned = pltpu.make_async_remote_copy(
            sbuf.at[q, pl.ds(0, NC - 1)], g.at[0, :, q, pl.ds(0, NC - 1)], s1.at[q], r1.at[q],
            device_id=to(UP), device_id_type=MESH,
        )
        turned.wait_recv()
        for src, dst, step in FIRST:
            push(src, dst, step, q)
        turned.wait_send()
    build_windows(blocks.at[0], lens, left)
    process(0)
    for q in range(NCH):
        for src, dst, step in second(q):
            push(src, dst, step, q)
    for slot in (4, 1, 3):
        process(slot)
    for q in range(NCH):
        push(*third(q), q)
    for slot in (2, 5, 7):
        process(slot)
    process_last(6, LT - 1)
    for cp in sends:
        cp.wait_send()


def store_kernel(vis_in, power_in, vis, power, sem):
    copies = [
        pltpu.make_async_copy(vis_in, vis, sem.at[0]),
        pltpu.make_async_copy(power_in, power, sem.at[1]),
    ]
    for cp in copies:
        cp.start()
    for cp in copies:
        cp.wait()


def store(vis, power):
    return pl.pallas_call(
        store_kernel,
        out_shape=(
            jax.ShapeDtypeStruct(vis.shape, vis.dtype),
            jax.ShapeDtypeStruct(power.shape, power.dtype),
        ),
        in_specs=[pl.BlockSpec(memory_space=pl.ANY)] * 2,
        out_specs=(pl.BlockSpec(memory_space=pltpu.HBM), pl.BlockSpec(memory_space=pltpu.HBM)),
        scratch_shapes=[pltpu.SemaphoreType.DMA((2,))],
        compiler_params=pltpu.CompilerParams(vmem_limit_bytes=VMEM_LIMIT),
        name="store",
    )(vis, power)


def local(voltages, phase_index, int_lengths, beam_weights):
    vis, power = pl.pallas_call(
        kernel,
        out_shape=(
            jax.ShapeDtypeStruct((1, OFFS, INTEG, 1, 2, BLK, BLK), BF),
            jax.ShapeDtypeStruct((INTEG, 1, SHARE), F32),
        ),
        in_specs=[
            pl.BlockSpec(memory_space=pltpu.HBM),
            pl.BlockSpec(memory_space=pltpu.HBM),
            pl.BlockSpec(memory_space=pltpu.HBM),
            pl.BlockSpec(memory_space=pltpu.HBM),
        ],
        out_specs=(pl.BlockSpec(memory_space=pltpu.VMEM), pl.BlockSpec(memory_space=pltpu.VMEM)),
        scratch_shapes=[
            pltpu.SMEM((INTEG,), jnp.int32),
            pltpu.SMEM((INTEG,), jnp.int32),
            pltpu.VMEM((NS, 2, LT, NC, 4, 128), BF),
            pltpu.VMEM((NC, 2, 4, SAMPLES), BF),
            pltpu.VMEM((LT, NC, 2, 4, 128), BF),
            pltpu.VMEM((NC, 8, 128), F32),
            pltpu.VMEM((2, SHARE, NS * BLK), BF),
            pltpu.VMEM((INTEG * BLK, 2 * SAMPLES), BF),
            pltpu.VMEM((2 * SHARE, SAMPLES), F32),
            pltpu.VMEM((INTEG * BLK, 2 * BLK), F32),
            pltpu.VMEM((8, SHARE), F32),
            pltpu.SemaphoreType.DMA((5,)),
            pltpu.SemaphoreType.DMA((NCH,)),
            pltpu.SemaphoreType.DMA((NCH,)),
            pltpu.SemaphoreType.DMA((NCH,)),
            pltpu.SemaphoreType.DMA((NS, NCH)),
            pltpu.SemaphoreType.DMA((NS, NCH)),
        ],
        compiler_params=pltpu.CompilerParams(
            collective_id=0, has_side_effects=True, vmem_limit_bytes=VMEM_LIMIT
        ),
        name="correlator",
    )(
        *[
            pltpu.with_memory_space_constraint(x, pltpu.HBM)
            for x in (phase_index, int_lengths, voltages, beam_weights)
        ]
    )
    return store(vis, power)


def solution(mesh):
    return jax.shard_map(
        local,
        mesh=mesh,
        in_specs=(P(None, None, ("stn", "chan"), None), P(("stn", "chan")), P(), P()),
        out_specs=(P("stn", None, None, "chan", None, None, None), P(None, "chan", "stn")),
        check_vma=False,
    )
```

```python
import functools
import math

import jax
import jax.numpy as jnp
from jax import lax
from jax.experimental import pallas as pl
from jax.experimental.pallas import tpu as pltpu
from jax.sharding import PartitionSpec as P

INTEG = 4
BEAMS = 256
PHASES = 1024
NC = 32
NS = 8
LT = 4
SAMPLES = 512
BLK = 128
OFFS = 5
SHARE = BEAMS // NS
NCH = LT
BF = jnp.bfloat16
FAR = sorted(range(1, NC), key=lambda k: -min(k % 16, 16 - k % 16))
F32 = jnp.float32
VMEM_LIMIT = 24 * 2**20
MESH = pl.DeviceIdType.MESH


def rotate_all(ph, vin, sbuf, trig):
    row = lax.broadcasted_iota(jnp.int32, (NC, 8, 128), 1)
    chan = lax.broadcasted_iota(jnp.int32, (NC, 8, 128), 0)
    col = row % 4
    step = jnp.where(col == 0, ph[0], jnp.where(col == 1, ph[1], jnp.where(col == 2, ph[2], ph[3])))
    turns = chan * step - jnp.where(row >= 4, PHASES // 4, 0)
    turns = ((turns + PHASES // 2) & (PHASES - 1)) - PHASES // 2
    trig[...] = jnp.cos(turns.astype(F32) * (2.0 * math.pi / PHASES))

    def one(c, carry):
        cs = trig[c]
        cos, sin = cs[0:4], cs[4:8]
        re = vin[c, 0].astype(F32)
        im = vin[c, 1].astype(F32)
        for t in range(LT):
            a = re[:, t * 128 : (t + 1) * 128]
            b = im[:, t * 128 : (t + 1) * 128]
            sbuf[t, c, 0] = (a * cos + b * sin).astype(BF)
            sbuf[t, c, 1] = (b * cos - a * sin).astype(BF)
        return carry

    lax.fori_loop(0, NC, one, 0, unroll=4)


def window_edges(lens):
    edges = [jnp.int32(0)]
    for j in range(INTEG):
        edges.append(edges[-1] + lens[j])
    return edges


def build_windows(blk, lens, left):
    edges = window_edges(lens)
    lane = lax.broadcasted_iota(jnp.int32, (1, 128), 1)
    for t in range(LT):
        at = lane + t * 128
        for j in range(INTEG):
            keep = ((at >= edges[j]) & (at < edges[j + 1])).astype(F32).astype(BF)
            for p in range(2):
                left[j * BLK : (j + 1) * BLK, (p * LT + t) * 128 : (p * LT + t + 1) * 128] = (
                    blk[p, t] * keep
                )


def products(blk, left, lo, hi):
    re = [blk[0, t] for t in range(lo, hi)]
    im = [blk[1, t] for t in range(lo, hi)]
    neg = [-x for x in im]
    right = jnp.concatenate(
        [jnp.concatenate(re + im, axis=1), jnp.concatenate(neg + re, axis=1)], axis=0
    )
    if (lo, hi) == (0, LT):
        rows = left[...]
    else:
        rows = jnp.concatenate(
            [left[:, (p * LT + lo) * 128 : (p * LT + hi) * 128] for p in range(2)], axis=1
        )
    return lax.dot_general(rows, right, (((1,), (1,)), ((), ())), preferred_element_type=F32)


def average(prod, lens, put):
    for j in range(INTEG):
        inverse = 1.0 / jnp.full((1, 128), lens[j], jnp.int32).astype(F32)
        for p in range(2):
            put(j, p, (prod[j * BLK : (j + 1) * BLK, p * 128 : (p + 1) * 128] * inverse).astype(BF))


def beam_part(blk, wts, dests, q, lo, hi):
    cols = pl.ds(pl.multiple_of(q * BLK, BLK), BLK)
    rows = []
    for d in dests:
        wr = wts[d, 0, :, cols]
        wi = wts[d, 1, :, cols]
        rows.append(jnp.concatenate([wr, -wi], axis=1))
        rows.append(jnp.concatenate([wi, wr], axis=1))
    stack = jnp.concatenate(rows, axis=0)
    parts = []
    for t in range(lo, hi, 2):
        x = jnp.concatenate(
            [jnp.concatenate([blk[p, u] for u in range(t, min(t + 2, hi))], axis=1) for p in range(2)],
            axis=0,
        )
        parts.append(jnp.dot(stack, x, preferred_element_type=F32))
    return jnp.concatenate(parts, axis=1)


def window_powers(beam, lens, lo):
    power = beam[:SHARE] ** 2 + beam[SHARE:] ** 2
    width = beam.shape[1]
    edges = window_edges(lens)
    at = lax.broadcasted_iota(jnp.int32, (8, width), 1) + lo * 128
    row = lax.broadcasted_iota(jnp.int32, (8, width), 0)
    mask = jnp.zeros((8, width), F32)
    for j in range(INTEG):
        inside = (row == j) & (at >= edges[j]) & (at < edges[j + 1])
        mask = jnp.where(inside, 1.0, mask)
    return lax.dot_general(
        mask, power, (((1,), (1,)), ((), ())), precision=lax.Precision.HIGHEST,
        preferred_element_type=F32,
    )


UP, DOWN, ACROSS = (0, 1), (0, -1), (1, 0)
FIRST = ((0, 4, ACROSS), (0, 1, UP), (0, 3, DOWN))
ROWS = 2 * SHARE


def kernel(
    ph_hbm, lens_hbm, v_hbm, w_hbm, vis, power,
    ph, lens, g, vin, sbuf, trig, wts, left, beam, acc, sums, out_part, in_part, lsem, o1, s1, r1, s2, r2, s3, r3,
):
    c = lax.axis_index("chan")
    s = lax.axis_index("stn")
    h, y = s // 4, s % 4

    def to(step):
        return {"chan": c, "stn": ((h + step[0]) % 2) * 4 + (y + step[1] + 4) % 4}

    barrier = pltpu.get_barrier_semaphore()

    for k in FAR:
        pl.semaphore_signal(
            barrier, 1, device_id={"chan": (c + k) % NC, "stn": s}, device_id_type=MESH
        )
    for step in (UP, DOWN, ACROSS):
        pl.semaphore_signal(barrier, 1, device_id=to(step), device_id_type=MESH)
    for k in (2, NS - 2):
        pl.semaphore_signal(
            barrier, 1, device_id={"chan": c, "stn": (s + k) % NS}, device_id_type=MESH
        )
    load = pltpu.make_async_copy(v_hbm, vin, lsem.at[0])
    load.start()
    load_p = pltpu.make_async_copy(ph_hbm, ph, lsem.at[3])
    load_p.start()
    load_l = pltpu.make_async_copy(lens_hbm, lens, lsem.at[4])
    load_l.start()
    load_w = [
        pltpu.make_async_copy(
            w_hbm.at[:, pl.ds(pl.multiple_of(d * SHARE, SHARE), SHARE)], wts.at[i], lsem.at[i + 1]
        )
        for i, d in enumerate((s, (s + 2) % NS))
    ]
    for cp in load_w:
        cp.start()
    load_p.wait()
    load.wait()
    rotate_all(ph, vin, sbuf, trig)
    pl.semaphore_wait(barrier, NC - 1 + 5)

    for q in range(NCH):
        for k in FAR:
            d = (c + k) % NC
            pltpu.make_async_remote_copy(
                sbuf.at[q, d], g.at[0, :, q, c], s1.at[q], r1.at[q],
                device_id={"chan": d, "stn": s}, device_id_type=MESH,
            ).start()
    owns = [
        pltpu.make_async_copy(sbuf.at[q, c], g.at[0, :, q, c], o1.at[q]) for q in range(NCH)
    ]
    for cp in owns:
        cp.start()
    for cp in owns:
        cp.wait()
    for cp in load_w:
        cp.wait()
    load_l.wait()

    sends = []
    have = {(0, q) for q in range(NCH)}

    def copy(src, dst, q, step):
        return pltpu.make_async_remote_copy(
            g.at[src, :, q], g.at[dst, :, q], s2.at[dst, q], r2.at[dst, q],
            device_id=to(step), device_id_type=MESH,
        )

    def arrive(slot, *chunks):
        for q in chunks:
            if (slot, q) not in have:
                copy(0, slot, q, UP).wait_recv()
                have.add((slot, q))

    def push(src, dst, step, q):
        arrive(src, q)
        cp = copy(src, dst, q, step)
        cp.start()
        sends.append(cp)

    blocks = g.reshape(NS, 2, LT, BLK, 128)

    def block_at(slot):
        dh, dy = slot // 4, slot % 4
        q = ((h + dh) % 2) * 4 + (y - dy + 4) % 4
        return q, (q - s + NS) % NS

    def process(slot):
        arrive(slot, *range(NCH))
        q, k = block_at(slot)
        part = beam_part(blocks.at[slot], wts, (0,), q, 0, LT)
        beam[...] += part

        @pl.when(k < OFFS)
        def _():
            vis_block(slot, k)

    def vis_block(slot, k):
        def put(j, p, value):
            vis[0, k, j, 0, p] = value

        average(products(blocks.at[slot], left, 0, LT), lens, put)

    middle = (y == 1) | (y == 2)
    part_copy = pltpu.make_async_remote_copy(
        out_part, in_part, s3, r3,
        device_id={"chan": c, "stn": (s + 2) % NS}, device_id_type=MESH,
    )

    spare_copy = pltpu.make_async_remote_copy(
        g.at[3, :, 2], g.at[2, :, 2], s2.at[6, 0], r2.at[2, 2],
        device_id=to(DOWN), device_id_type=MESH,
    )

    for q in range(NCH):
        turned = pltpu.make_async_remote_copy(
            sbuf.at[q, pl.ds(0, NC - 1)], g.at[0, :, q, pl.ds(0, NC - 1)], s1.at[q], r1.at[q],
            device_id=to(UP), device_id_type=MESH,
        )
        turned.wait_recv()
        for src, dst, step in FIRST:
            push(src, dst, step, q)
        turned.wait_send()
    part = beam_part(blocks.at[0], wts, (0, 1), s, 0, LT)
    beam[...] = part[:ROWS]
    out_part[...] = part[ROWS:].astype(BF)
    build_windows(blocks.at[0], lens, left)
    vis_block(0, 0)
    part_copy.start()
    for q in range(NCH):
        if q % 2 == 0:
            push(3, 7, ACROSS, q)
            push(4, 5, UP, q)
        else:
            push(1, 5, ACROSS, q)
            push(4, 7, DOWN, q)
    for q in range(NCH):
        arrive(1 if q % 2 == 0 else 3, q)

        sender = (y == 0) if q == 2 else ~middle if q % 2 == 0 else middle

        @pl.when(sender)
        def _():
            if q % 2 == 0:
                copy(1, 2, q, UP).start()
            else:
                copy(3, 2, q, DOWN).start()

        if q == 2:
            arrive(3, q)
            pl.when(y == 1)(spare_copy.start)

    def last_hop(q):
        if q % 2 == 0:
            arrive(5, q)

            @pl.when(middle)
            def _():
                copy(5, 2, q, UP).start()
        else:
            arrive(7, q)

            @pl.when(~middle)
            def _():
                copy(7, 2, q, DOWN).start()

    process(4)
    process(1)
    last_hop(0)
    last_hop(1)
    process(3)
    last_hop(2)
    last_hop(3)
    process(7)
    process(5)
    cut = LT - 1
    late = (s + 2) % NS
    arrive(2, *range(cut))
    acc[...] = products(blocks.at[2], left, 0, cut)
    part_copy.wait_recv()
    beam[...] += in_part[...].astype(F32)
    head = beam[:, : cut * 128] + beam_part(blocks.at[2], wts, (0,), late, 0, cut)
    sums[...] = window_powers(head, lens, 0)
    arrive(2, cut)
    rest = beam[:, cut * 128 :] + beam_part(blocks.at[2], wts, (0,), late, cut, LT)
    total = sums[...] + window_powers(rest, lens, cut)
    for j in range(INTEG):
        power[j] = total[j : j + 1] / jnp.full((1, SHARE), lens[j], jnp.int32).astype(F32)

    def put(j, p, value):
        vis[0, 2, j, 0, p] = value

    average(acc[...] + products(blocks.at[2], left, cut, LT), lens, put)
    for cp in sends:
        cp.wait_send()
    for q in range(NCH):
        if q == 2:
            pl.when(y < 3)(copy(0, 2, q, UP).wait_send)
        else:
            copy(0, 2, q, UP).wait_send()
    pl.when(y == 1)(spare_copy.wait_send)
    part_copy.wait_send()


def store_kernel(vis_in, power_in, vis, power, sem):
    copies = [
        pltpu.make_async_copy(vis_in, vis, sem.at[0]),
        pltpu.make_async_copy(power_in, power, sem.at[1]),
    ]
    for cp in copies:
        cp.start()
    for cp in copies:
        cp.wait()


def store(vis, power):
    return pl.pallas_call(
        store_kernel,
        out_shape=(
            jax.ShapeDtypeStruct(vis.shape, vis.dtype),
            jax.ShapeDtypeStruct(power.shape, power.dtype),
        ),
        in_specs=[pl.BlockSpec(memory_space=pl.ANY)] * 2,
        out_specs=(pl.BlockSpec(memory_space=pltpu.HBM), pl.BlockSpec(memory_space=pltpu.HBM)),
        scratch_shapes=[pltpu.SemaphoreType.DMA((2,))],
        compiler_params=pltpu.CompilerParams(vmem_limit_bytes=VMEM_LIMIT),
        name="store",
    )(vis, power)


def local(voltages, phase_index, int_lengths, beam_weights):
    vis, power = pl.pallas_call(
        kernel,
        out_shape=(
            jax.ShapeDtypeStruct((1, OFFS, INTEG, 1, 2, BLK, BLK), BF),
            jax.ShapeDtypeStruct((INTEG, 1, SHARE), F32),
        ),
        in_specs=[
            pl.BlockSpec(memory_space=pltpu.HBM),
            pl.BlockSpec(memory_space=pltpu.HBM),
            pl.BlockSpec(memory_space=pltpu.HBM),
            pl.BlockSpec(memory_space=pltpu.HBM),
        ],
        out_specs=(pl.BlockSpec(memory_space=pltpu.VMEM), pl.BlockSpec(memory_space=pltpu.VMEM)),
        scratch_shapes=[
            pltpu.SMEM((INTEG,), jnp.int32),
            pltpu.SMEM((INTEG,), jnp.int32),
            pltpu.VMEM((NS, 2, LT, NC, 4, 128), BF),
            pltpu.VMEM((NC, 2, 4, SAMPLES), BF),
            pltpu.VMEM((LT, NC, 2, 4, 128), BF),
            pltpu.VMEM((NC, 8, 128), F32),
            pltpu.VMEM((2, 2, SHARE, NS * BLK), BF),
            pltpu.VMEM((INTEG * BLK, 2 * SAMPLES), BF),
            pltpu.VMEM((2 * SHARE, SAMPLES), F32),
            pltpu.VMEM((INTEG * BLK, 2 * BLK), F32),
            pltpu.VMEM((8, SHARE), F32),
            pltpu.VMEM((ROWS, SAMPLES), BF),
            pltpu.VMEM((ROWS, SAMPLES), BF),
            pltpu.SemaphoreType.DMA((5,)),
            pltpu.SemaphoreType.DMA((NCH,)),
            pltpu.SemaphoreType.DMA((NCH,)),
            pltpu.SemaphoreType.DMA((NCH,)),
            pltpu.SemaphoreType.DMA((NS, NCH)),
            pltpu.SemaphoreType.DMA((NS, NCH)),
            pltpu.SemaphoreType.DMA,
            pltpu.SemaphoreType.DMA,
        ],
        compiler_params=pltpu.CompilerParams(
            collective_id=0, has_side_effects=True, vmem_limit_bytes=VMEM_LIMIT
        ),
        name="correlator",
    )(
        *[
            pltpu.with_memory_space_constraint(x, pltpu.HBM)
            for x in (phase_index, int_lengths, voltages, beam_weights)
        ]
    )
    return store(vis, power)


def solution(mesh):
    return jax.shard_map(
        local,
        mesh=mesh,
        in_specs=(P(None, None, ("stn", "chan"), None), P(("stn", "chan")), P(), P()),
        out_specs=(P("stn", None, None, "chan", None, None, None), P(None, "chan", "stn")),
        check_vma=False,
    )
```

```python
import functools
import math

import jax
import jax.numpy as jnp
from jax import lax
from jax.experimental import pallas as pl
from jax.experimental.pallas import tpu as pltpu
from jax.sharding import PartitionSpec as P

INTEG = 4
BEAMS = 256
PHASES = 1024
NC = 32
NS = 8
LT = 4
SAMPLES = 512
BLK = 128
OFFS = 5
SHARE = BEAMS // NS
NCH = LT
BF = jnp.bfloat16
FAR = sorted(range(1, NC), key=lambda k: -min(k % 16, 16 - k % 16))
F32 = jnp.float32
VMEM_LIMIT = 24 * 2**20
MESH = pl.DeviceIdType.MESH


def rotate_all(ph, vin, sbuf, trig):
    row = lax.broadcasted_iota(jnp.int32, (NC, 8, 128), 1)
    chan = lax.broadcasted_iota(jnp.int32, (NC, 8, 128), 0)
    col = row % 4
    step = jnp.where(col == 0, ph[0], jnp.where(col == 1, ph[1], jnp.where(col == 2, ph[2], ph[3])))
    turns = chan * step - jnp.where(row >= 4, PHASES // 4, 0)
    turns = ((turns + PHASES // 2) & (PHASES - 1)) - PHASES // 2
    trig[...] = jnp.cos(turns.astype(F32) * (2.0 * math.pi / PHASES))

    def one(c, carry):
        cs = trig[c]
        cos, sin = cs[0:4], cs[4:8]
        re = vin[c, 0].astype(F32)
        im = vin[c, 1].astype(F32)
        for t in range(LT):
            a = re[:, t * 128 : (t + 1) * 128]
            b = im[:, t * 128 : (t + 1) * 128]
            sbuf[t, c, 0] = (a * cos + b * sin).astype(BF)
            sbuf[t, c, 1] = (b * cos - a * sin).astype(BF)
        return carry

    lax.fori_loop(0, NC, one, 0, unroll=4)


def window_edges(lens):
    edges = [jnp.int32(0)]
    for j in range(INTEG):
        edges.append(edges[-1] + lens[j])
    return edges


def build_windows(blk, lens, left):
    edges = window_edges(lens)
    lane = lax.broadcasted_iota(jnp.int32, (1, 128), 1)
    for t in range(LT):
        at = lane + t * 128
        for j in range(INTEG):
            keep = ((at >= edges[j]) & (at < edges[j + 1])).astype(F32).astype(BF)
            for p in range(2):
                left[j * BLK : (j + 1) * BLK, (p * LT + t) * 128 : (p * LT + t + 1) * 128] = (
                    blk[p, t] * keep
                )


def products(blk, left, lo, hi):
    re = [blk[0, t] for t in range(lo, hi)]
    im = [blk[1, t] for t in range(lo, hi)]
    neg = [-x for x in im]
    right = jnp.concatenate(
        [jnp.concatenate(re + im, axis=1), jnp.concatenate(neg + re, axis=1)], axis=0
    )
    if (lo, hi) == (0, LT):
        rows = left[...]
    else:
        rows = jnp.concatenate(
            [left[:, (p * LT + lo) * 128 : (p * LT + hi) * 128] for p in range(2)], axis=1
        )
    return lax.dot_general(rows, right, (((1,), (1,)), ((), ())), preferred_element_type=F32)


def average(prod, lens, put):
    for j in range(INTEG):
        inverse = 1.0 / jnp.full((1, 128), lens[j], jnp.int32).astype(F32)
        for p in range(2):
            put(j, p, (prod[j * BLK : (j + 1) * BLK, p * 128 : (p + 1) * 128] * inverse).astype(BF))


def beam_part(blk, wts, dests, q, lo, hi):
    cols = pl.ds(pl.multiple_of(q * BLK, BLK), BLK)
    rows = []
    for d in dests:
        wr = wts[d, 0, :, cols]
        wi = wts[d, 1, :, cols]
        rows.append(jnp.concatenate([wr, -wi], axis=1))
        rows.append(jnp.concatenate([wi, wr], axis=1))
    stack = jnp.concatenate(rows, axis=0)
    parts = []
    for t in range(lo, hi, 2):
        x = jnp.concatenate(
            [jnp.concatenate([blk[p, u] for u in range(t, min(t + 2, hi))], axis=1) for p in range(2)],
            axis=0,
        )
        parts.append(jnp.dot(stack, x, preferred_element_type=F32))
    return jnp.concatenate(parts, axis=1)


def window_powers(beam, lens, lo):
    power = beam[:SHARE] ** 2 + beam[SHARE:] ** 2
    width = beam.shape[1]
    edges = window_edges(lens)
    at = lax.broadcasted_iota(jnp.int32, (8, width), 1) + lo * 128
    row = lax.broadcasted_iota(jnp.int32, (8, width), 0)
    mask = jnp.zeros((8, width), F32)
    for j in range(INTEG):
        inside = (row == j) & (at >= edges[j]) & (at < edges[j + 1])
        mask = jnp.where(inside, 1.0, mask)
    return lax.dot_general(
        mask, power, (((1,), (1,)), ((), ())), precision=lax.Precision.HIGHEST,
        preferred_element_type=F32,
    )


UP, DOWN, ACROSS = (0, 1), (0, -1), (1, 0)
FIRST = ((0, 4, ACROSS), (0, 1, UP), (0, 3, DOWN))
ROWS = 2 * SHARE


def kernel(
    ph_hbm, lens_hbm, v_hbm, w_hbm, vis, power,
    ph, lens, g, vin, sbuf, trig, wts, left, beam, acc, sums, out_part, in_part, lsem, o1, s1, r1, s2, r2, s3, r3,
):
    c = lax.axis_index("chan")
    s = lax.axis_index("stn")
    h, y = s // 4, s % 4

    def to(step):
        return {"chan": c, "stn": ((h + step[0]) % 2) * 4 + (y + step[1] + 4) % 4}

    barrier = pltpu.get_barrier_semaphore()

    for k in FAR:
        pl.semaphore_signal(
            barrier, 1, device_id={"chan": (c + k) % NC, "stn": s}, device_id_type=MESH
        )
    for step in (UP, DOWN, ACROSS):
        pl.semaphore_signal(barrier, 1, device_id=to(step), device_id_type=MESH)
    for k in (2, NS - 2):
        pl.semaphore_signal(
            barrier, 1, device_id={"chan": c, "stn": (s + k) % NS}, device_id_type=MESH
        )
    load = pltpu.make_async_copy(v_hbm, vin, lsem.at[0])
    load.start()
    load_p = pltpu.make_async_copy(ph_hbm, ph, lsem.at[3])
    load_p.start()
    load_l = pltpu.make_async_copy(lens_hbm, lens, lsem.at[4])
    load_l.start()
    load_w = [
        pltpu.make_async_copy(
            w_hbm.at[:, pl.ds(pl.multiple_of(d * SHARE, SHARE), SHARE)], wts.at[i], lsem.at[i + 1]
        )
        for i, d in enumerate((s, (s + 2) % NS))
    ]
    for cp in load_w:
        cp.start()
    load_p.wait()
    load.wait()
    rotate_all(ph, vin, sbuf, trig)
    pl.semaphore_wait(barrier, NC - 1 + 5)

    for q in range(NCH):
        for k in FAR:
            d = (c + k) % NC
            pltpu.make_async_remote_copy(
                sbuf.at[q, d], g.at[0, :, q, c], s1.at[q], r1.at[q],
                device_id={"chan": d, "stn": s}, device_id_type=MESH,
            ).start()
    owns = [
        pltpu.make_async_copy(sbuf.at[q, c], g.at[0, :, q, c], o1.at[q]) for q in range(NCH)
    ]
    for cp in owns:
        cp.start()
    for cp in owns:
        cp.wait()
    for cp in load_w:
        cp.wait()
    load_l.wait()

    sends = []
    have = {(0, q) for q in range(NCH)}

    def copy(src, dst, q, step):
        return pltpu.make_async_remote_copy(
            g.at[src, :, q], g.at[dst, :, q], s2.at[dst, q], r2.at[dst, q],
            device_id=to(step), device_id_type=MESH,
        )

    def arrive(slot, *chunks):
        for q in chunks:
            if (slot, q) not in have:
                copy(0, slot, q, UP).wait_recv()
                have.add((slot, q))

    def push(src, dst, step, q):
        arrive(src, q)
        cp = copy(src, dst, q, step)
        cp.start()
        sends.append(cp)

    blocks = g.reshape(NS, 2, LT, BLK, 128)

    def block_at(slot):
        dh, dy = slot // 4, slot % 4
        q = ((h + dh) % 2) * 4 + (y - dy + 4) % 4
        return q, (q - s + NS) % NS

    def process(slot):
        arrive(slot, *range(NCH))
        q, k = block_at(slot)
        part = beam_part(blocks.at[slot], wts, (0,), q, 0, LT)
        beam[...] += part

        @pl.when(k < OFFS)
        def _():
            vis_block(slot, k)

    def vis_block(slot, k):
        def put(j, p, value):
            vis[0, k, j, 0, p] = value

        average(products(blocks.at[slot], left, 0, LT), lens, put)

    middle = (y == 1) | (y == 2)
    part_copy = pltpu.make_async_remote_copy(
        out_part, in_part, s3, r3,
        device_id={"chan": c, "stn": (s + 2) % NS}, device_id_type=MESH,
    )

    fifth_copy = pltpu.make_async_remote_copy(
        g.at[4, :, NCH - 1], g.at[5, :, NCH - 1], s2.at[6, 1], r2.at[5, NCH - 1],
        device_id=to(UP), device_id_type=MESH,
    )
    spare_copy = pltpu.make_async_remote_copy(
        g.at[3, :, 2], g.at[2, :, 2], s2.at[6, 0], r2.at[2, 2],
        device_id=to(DOWN), device_id_type=MESH,
    )

    for q in range(NCH):
        turned = pltpu.make_async_remote_copy(
            sbuf.at[q, pl.ds(0, NC - 1)], g.at[0, :, q, pl.ds(0, NC - 1)], s1.at[q], r1.at[q],
            device_id=to(UP), device_id_type=MESH,
        )
        turned.wait_recv()
        for src, dst, step in FIRST:
            push(src, dst, step, q)
        turned.wait_send()
    part = beam_part(blocks.at[0], wts, (0, 1), s, 0, LT)
    beam[...] = part[:ROWS]
    out_part[...] = part[ROWS:].astype(BF)
    build_windows(blocks.at[0], lens, left)
    vis_block(0, 0)
    part_copy.start()
    for q in range(NCH):
        if q % 2 == 0:
            push(3, 7, ACROSS, q)
            push(4, 5, UP, q)
        else:
            if q < NCH - 1:
                push(1, 5, ACROSS, q)
            else:
                arrive(1, q)
                pl.when(y < 2)(copy(1, 5, q, ACROSS).start)
            push(4, 7, DOWN, q)
            if q == NCH - 1:
                pl.when(middle)(fifth_copy.start)
    for q in range(NCH):
        arrive(1 if q % 2 == 0 else 3, q)

        sender = (y == 0) if q == 2 else ~middle if q % 2 == 0 else middle

        @pl.when(sender)
        def _():
            if q % 2 == 0:
                copy(1, 2, q, UP).start()
            else:
                copy(3, 2, q, DOWN).start()

        if q == 2:
            arrive(3, q)
            pl.when(y == 1)(spare_copy.start)

    def last_hop(q):
        if q % 2 == 0:
            arrive(5, q)

            @pl.when(middle)
            def _():
                copy(5, 2, q, UP).start()
        else:
            arrive(7, q)

            @pl.when(~middle)
            def _():
                copy(7, 2, q, DOWN).start()

    process(4)
    process(1)
    last_hop(0)
    last_hop(1)
    process(3)
    last_hop(2)
    last_hop(3)
    process(7)
    q5, k5 = block_at(5)
    arrive(5, 0, 1, 2)
    beam[:, : 3 * 128] += beam_part(blocks.at[5], wts, (0,), q5, 0, 3)
    arrive(5, 3)
    beam[:, 3 * 128 :] += beam_part(blocks.at[5], wts, (0,), q5, 3, LT)

    @pl.when(k5 < OFFS)
    def _():
        vis_block(5, k5)

    part_copy.wait_recv()
    beam[...] += in_part[...].astype(F32)
    cut = LT - 1
    late = (s + 2) % NS
    arrive(2, *range(cut))
    acc[...] = products(blocks.at[2], left, 0, cut)
    head = beam[:, : cut * 128] + beam_part(blocks.at[2], wts, (0,), late, 0, cut)
    sums[...] = window_powers(head, lens, 0)
    arrive(2, cut)
    rest = beam[:, cut * 128 :] + beam_part(blocks.at[2], wts, (0,), late, cut, LT)
    total = sums[...] + window_powers(rest, lens, cut)
    for j in range(INTEG):
        power[j] = total[j : j + 1] / jnp.full((1, SHARE), lens[j], jnp.int32).astype(F32)

    def put(j, p, value):
        vis[0, 2, j, 0, p] = value

    average(acc[...] + products(blocks.at[2], left, cut, LT), lens, put)
    for cp in sends:
        cp.wait_send()
    for q in range(NCH):
        if q == 2:
            pl.when(y < 3)(copy(0, 2, q, UP).wait_send)
        else:
            copy(0, 2, q, UP).wait_send()
    pl.when(y == 1)(spare_copy.wait_send)
    pl.when(y < 2)(copy(1, 5, NCH - 1, ACROSS).wait_send)
    pl.when(middle)(fifth_copy.wait_send)
    part_copy.wait_send()


def store_kernel(vis_in, power_in, vis, power, sem):
    copies = [
        pltpu.make_async_copy(vis_in, vis, sem.at[0]),
        pltpu.make_async_copy(power_in, power, sem.at[1]),
    ]
    for cp in copies:
        cp.start()
    for cp in copies:
        cp.wait()


def store(vis, power):
    return pl.pallas_call(
        store_kernel,
        out_shape=(
            jax.ShapeDtypeStruct(vis.shape, vis.dtype),
            jax.ShapeDtypeStruct(power.shape, power.dtype),
        ),
        in_specs=[pl.BlockSpec(memory_space=pl.ANY)] * 2,
        out_specs=(pl.BlockSpec(memory_space=pltpu.HBM), pl.BlockSpec(memory_space=pltpu.HBM)),
        scratch_shapes=[pltpu.SemaphoreType.DMA((2,))],
        compiler_params=pltpu.CompilerParams(vmem_limit_bytes=VMEM_LIMIT),
        name="store",
    )(vis, power)


def local(voltages, phase_index, int_lengths, beam_weights):
    vis, power = pl.pallas_call(
        kernel,
        out_shape=(
            jax.ShapeDtypeStruct((1, OFFS, INTEG, 1, 2, BLK, BLK), BF),
            jax.ShapeDtypeStruct((INTEG, 1, SHARE), F32),
        ),
        in_specs=[
            pl.BlockSpec(memory_space=pltpu.HBM),
            pl.BlockSpec(memory_space=pltpu.HBM),
            pl.BlockSpec(memory_space=pltpu.HBM),
            pl.BlockSpec(memory_space=pltpu.HBM),
        ],
        out_specs=(pl.BlockSpec(memory_space=pltpu.VMEM), pl.BlockSpec(memory_space=pltpu.VMEM)),
        scratch_shapes=[
            pltpu.SMEM((INTEG,), jnp.int32),
            pltpu.SMEM((INTEG,), jnp.int32),
            pltpu.VMEM((NS, 2, LT, NC, 4, 128), BF),
            pltpu.VMEM((NC, 2, 4, SAMPLES), BF),
            pltpu.VMEM((LT, NC, 2, 4, 128), BF),
            pltpu.VMEM((NC, 8, 128), F32),
            pltpu.VMEM((2, 2, SHARE, NS * BLK), BF),
            pltpu.VMEM((INTEG * BLK, 2 * SAMPLES), BF),
            pltpu.VMEM((2 * SHARE, SAMPLES), F32),
            pltpu.VMEM((INTEG * BLK, 2 * BLK), F32),
            pltpu.VMEM((8, SHARE), F32),
            pltpu.VMEM((ROWS, SAMPLES), BF),
            pltpu.VMEM((ROWS, SAMPLES), BF),
            pltpu.SemaphoreType.DMA((5,)),
            pltpu.SemaphoreType.DMA((NCH,)),
            pltpu.SemaphoreType.DMA((NCH,)),
            pltpu.SemaphoreType.DMA((NCH,)),
            pltpu.SemaphoreType.DMA((NS, NCH)),
            pltpu.SemaphoreType.DMA((NS, NCH)),
            pltpu.SemaphoreType.DMA,
            pltpu.SemaphoreType.DMA,
        ],
        compiler_params=pltpu.CompilerParams(
            collective_id=0, has_side_effects=True, vmem_limit_bytes=VMEM_LIMIT
        ),
        name="correlator",
    )(
        *[
            pltpu.with_memory_space_constraint(x, pltpu.HBM)
            for x in (phase_index, int_lengths, voltages, beam_weights)
        ]
    )
    return store(vis, power)


def solution(mesh):
    return jax.shard_map(
        local,
        mesh=mesh,
        in_specs=(P(None, None, ("stn", "chan"), None), P(("stn", "chan")), P(), P()),
        out_specs=(P("stn", None, None, "chan", None, None, None), P(None, "chan", "stn")),
        check_vma=False,
    )
```

```python
import functools
import math

import jax
import jax.numpy as jnp
from jax import lax
from jax.experimental import pallas as pl
from jax.experimental.pallas import tpu as pltpu
from jax.sharding import PartitionSpec as P

INTEG = 4
BEAMS = 256
PHASES = 1024
NC = 32
NS = 8
LT = 4
SAMPLES = 512
BLK = 128
OFFS = 5
SHARE = BEAMS // NS
NCH = LT
BF = jnp.bfloat16
FAR = sorted(range(1, NC), key=lambda k: -min(k % 16, 16 - k % 16))
F32 = jnp.float32
VMEM_LIMIT = 24 * 2**20
MESH = pl.DeviceIdType.MESH


def rotate_all(ph, vin, sbuf, trig):
    row = lax.broadcasted_iota(jnp.int32, (NC, 8, 128), 1)
    chan = lax.broadcasted_iota(jnp.int32, (NC, 8, 128), 0)
    col = row % 4
    step = jnp.where(col == 0, ph[0], jnp.where(col == 1, ph[1], jnp.where(col == 2, ph[2], ph[3])))
    turns = chan * step - jnp.where(row >= 4, PHASES // 4, 0)
    turns = ((turns + PHASES // 2) & (PHASES - 1)) - PHASES // 2
    trig[...] = jnp.cos(turns.astype(F32) * (2.0 * math.pi / PHASES))

    def one(c, carry):
        cs = trig[c]
        cos, sin = cs[0:4], cs[4:8]
        re = vin[c, 0].astype(F32)
        im = vin[c, 1].astype(F32)
        for t in range(LT):
            a = re[:, t * 128 : (t + 1) * 128]
            b = im[:, t * 128 : (t + 1) * 128]
            sbuf[t, c, 0] = (a * cos + b * sin).astype(BF)
            sbuf[t, c, 1] = (b * cos - a * sin).astype(BF)
        return carry

    lax.fori_loop(0, NC, one, 0, unroll=4)


def window_edges(lens):
    edges = [jnp.int32(0)]
    for j in range(INTEG):
        edges.append(edges[-1] + lens[j])
    return edges


def build_windows(blk, lens, left):
    edges = window_edges(lens)
    lane = lax.broadcasted_iota(jnp.int32, (1, 128), 1)
    for t in range(LT):
        at = lane + t * 128
        for j in range(INTEG):
            keep = ((at >= edges[j]) & (at < edges[j + 1])).astype(F32).astype(BF)
            for p in range(2):
                left[j * BLK : (j + 1) * BLK, (p * LT + t) * 128 : (p * LT + t + 1) * 128] = (
                    blk[p, t] * keep
                )


def products(blk, left, lo, hi):
    re = [blk[0, t] for t in range(lo, hi)]
    im = [blk[1, t] for t in range(lo, hi)]
    neg = [-x for x in im]
    right = jnp.concatenate(
        [jnp.concatenate(re + im, axis=1), jnp.concatenate(neg + re, axis=1)], axis=0
    )
    if (lo, hi) == (0, LT):
        rows = left[...]
    else:
        rows = jnp.concatenate(
            [left[:, (p * LT + lo) * 128 : (p * LT + hi) * 128] for p in range(2)], axis=1
        )
    return lax.dot_general(rows, right, (((1,), (1,)), ((), ())), preferred_element_type=F32)


def average(prod, lens, put):
    for j in range(INTEG):
        inverse = 1.0 / jnp.full((1, 128), lens[j], jnp.int32).astype(F32)
        for p in range(2):
            put(j, p, (prod[j * BLK : (j + 1) * BLK, p * 128 : (p + 1) * 128] * inverse).astype(BF))


def beam_part(blk, wts, dests, q, lo, hi):
    cols = pl.ds(pl.multiple_of(q * BLK, BLK), BLK)
    rows = []
    for d in dests:
        wr = wts[d, 0, :, cols]
        wi = wts[d, 1, :, cols]
        rows.append(jnp.concatenate([wr, -wi], axis=1))
        rows.append(jnp.concatenate([wi, wr], axis=1))
    stack = jnp.concatenate(rows, axis=0)
    parts = []
    for t in range(lo, hi, 2):
        x = jnp.concatenate(
            [jnp.concatenate([blk[p, u] for u in range(t, min(t + 2, hi))], axis=1) for p in range(2)],
            axis=0,
        )
        parts.append(jnp.dot(stack, x, preferred_element_type=F32))
    return jnp.concatenate(parts, axis=1)


def window_powers(beam, lens, lo):
    power = beam[:SHARE] ** 2 + beam[SHARE:] ** 2
    width = beam.shape[1]
    edges = window_edges(lens)
    at = lax.broadcasted_iota(jnp.int32, (8, width), 1) + lo * 128
    row = lax.broadcasted_iota(jnp.int32, (8, width), 0)
    mask = jnp.zeros((8, width), F32)
    for j in range(INTEG):
        inside = (row == j) & (at >= edges[j]) & (at < edges[j + 1])
        mask = jnp.where(inside, 1.0, mask)
    return lax.dot_general(
        mask, power, (((1,), (1,)), ((), ())), precision=lax.Precision.HIGHEST,
        preferred_element_type=F32,
    )


UP, DOWN, ACROSS = (0, 1), (0, -1), (1, 0)
FIRST = ((0, 1, UP), (0, 3, DOWN), (0, 4, ACROSS))
ROWS = 2 * SHARE


def kernel(
    ph_hbm, lens_hbm, v_hbm, w_hbm, vis, power,
    ph, lens, g, vin, sbuf, trig, wts, left, beam, acc, sums, out_part, in_part, lsem, o1, s1, r1, s2, r2, s3, r3,
):
    c = lax.axis_index("chan")
    s = lax.axis_index("stn")
    h, y = s // 4, s % 4

    def to(step):
        return {"chan": c, "stn": ((h + step[0]) % 2) * 4 + (y + step[1] + 4) % 4}

    barrier = pltpu.get_barrier_semaphore()

    for k in FAR[:8]:
        pl.semaphore_signal(
            barrier, 1, device_id={"chan": (c + k) % NC, "stn": s}, device_id_type=MESH
        )
    for step in (UP, DOWN, ACROSS):
        pl.semaphore_signal(barrier, 1, device_id=to(step), device_id_type=MESH)
    for k in (2, NS - 2):
        pl.semaphore_signal(
            barrier, 1, device_id={"chan": c, "stn": (s + k) % NS}, device_id_type=MESH
        )
    for k in FAR[8:]:
        pl.semaphore_signal(
            barrier, 1, device_id={"chan": (c + k) % NC, "stn": s}, device_id_type=MESH
        )
    load = pltpu.make_async_copy(v_hbm, vin, lsem.at[0])
    load.start()
    load_p = pltpu.make_async_copy(ph_hbm, ph, lsem.at[3])
    load_p.start()
    load_l = pltpu.make_async_copy(lens_hbm, lens, lsem.at[4])
    load_l.start()
    load_w = [
        pltpu.make_async_copy(
            w_hbm.at[:, pl.ds(pl.multiple_of(d * SHARE, SHARE), SHARE)], wts.at[i], lsem.at[i + 1]
        )
        for i, d in enumerate((s, (s + 2) % NS))
    ]
    for cp in load_w:
        cp.start()
    load_p.wait()
    load.wait()
    rotate_all(ph, vin, sbuf, trig)
    pl.semaphore_wait(barrier, NC - 1 + 5)

    for q in range(NCH):
        for k in FAR:
            d = (c + k) % NC
            pltpu.make_async_remote_copy(
                sbuf.at[q, d], g.at[0, :, q, c], s1.at[q], r1.at[q],
                device_id={"chan": d, "stn": s}, device_id_type=MESH,
            ).start()
    owns = [
        pltpu.make_async_copy(sbuf.at[q, c], g.at[0, :, q, c], o1.at[q]) for q in range(NCH)
    ]
    for cp in owns:
        cp.start()
    for cp in owns:
        cp.wait()
    for cp in load_w:
        cp.wait()
    load_l.wait()

    sends = []
    have = {(0, q) for q in range(NCH)}

    def copy(src, dst, q, step):
        return pltpu.make_async_remote_copy(
            g.at[src, :, q], g.at[dst, :, q], s2.at[dst, q], r2.at[dst, q],
            device_id=to(step), device_id_type=MESH,
        )

    def arrive(slot, *chunks):
        for q in chunks:
            if (slot, q) not in have:
                copy(0, slot, q, UP).wait_recv()
                have.add((slot, q))

    def push(src, dst, step, q):
        arrive(src, q)
        cp = copy(src, dst, q, step)
        cp.start()
        sends.append(cp)

    blocks = g.reshape(NS, 2, LT, BLK, 128)

    def block_at(slot):
        dh, dy = slot // 4, slot % 4
        q = ((h + dh) % 2) * 4 + (y - dy + 4) % 4
        return q, (q - s + NS) % NS

    def process(slot):
        arrive(slot, *range(NCH))
        q, k = block_at(slot)
        part = beam_part(blocks.at[slot], wts, (0,), q, 0, LT)
        beam[...] += part

        @pl.when(k < OFFS)
        def _():
            vis_block(slot, k)

    def vis_block(slot, k):
        def put(j, p, value):
            vis[0, k, j, 0, p] = value

        average(products(blocks.at[slot], left, 0, LT), lens, put)

    middle = (y == 1) | (y == 2)
    part_copy = pltpu.make_async_remote_copy(
        out_part, in_part, s3, r3,
        device_id={"chan": c, "stn": (s + 2) % NS}, device_id_type=MESH,
    )

    fifth_copy = pltpu.make_async_remote_copy(
        g.at[4, :, NCH - 1], g.at[5, :, NCH - 1], s2.at[6, 1], r2.at[5, NCH - 1],
        device_id=to(UP), device_id_type=MESH,
    )
    spare_copy = pltpu.make_async_remote_copy(
        g.at[3, :, 2], g.at[2, :, 2], s2.at[6, 0], r2.at[2, 2],
        device_id=to(DOWN), device_id_type=MESH,
    )

    for q in range(NCH):
        turned = pltpu.make_async_remote_copy(
            sbuf.at[q, pl.ds(0, NC - 1)], g.at[0, :, q, pl.ds(0, NC - 1)], s1.at[q], r1.at[q],
            device_id=to(UP), device_id_type=MESH,
        )
        turned.wait_recv()
        for src, dst, step in FIRST:
            push(src, dst, step, q)
        turned.wait_send()
    part = beam_part(blocks.at[0], wts, (0, 1), s, 0, LT)
    beam[...] = part[:ROWS]
    out_part[...] = part[ROWS:].astype(BF)
    build_windows(blocks.at[0], lens, left)
    vis_block(0, 0)
    part_copy.start()
    for q in range(NCH):
        if q % 2 == 0:
            push(3, 7, ACROSS, q)
            push(4, 5, UP, q)
        else:
            if q < NCH - 1:
                push(1, 5, ACROSS, q)
            else:
                arrive(1, q)
                pl.when(y < 2)(copy(1, 5, q, ACROSS).start)
            push(4, 7, DOWN, q)
            if q == NCH - 1:
                pl.when(middle)(fifth_copy.start)
    for q in range(NCH):
        arrive(1 if q % 2 == 0 else 3, q)

        sender = (y == 0) if q == 2 else ~middle if q % 2 == 0 else middle

        @pl.when(sender)
        def _():
            if q % 2 == 0:
                copy(1, 2, q, UP).start()
            else:
                copy(3, 2, q, DOWN).start()

        if q == 2:
            arrive(3, q)
            pl.when(y == 1)(spare_copy.start)

    def last_hop(q):
        if q % 2 == 0:
            arrive(5, q)

            @pl.when(middle)
            def _():
                copy(5, 2, q, UP).start()
        else:
            arrive(7, q)

            @pl.when(~middle)
            def _():
                copy(7, 2, q, DOWN).start()

    process(4)
    process(1)
    last_hop(0)
    last_hop(1)
    process(3)
    last_hop(2)
    last_hop(3)
    process(7)
    q5, k5 = block_at(5)
    arrive(5, 0, 1, 2)
    beam[:, : 3 * 128] += beam_part(blocks.at[5], wts, (0,), q5, 0, 3)
    arrive(5, 3)
    beam[:, 3 * 128 :] += beam_part(blocks.at[5], wts, (0,), q5, 3, LT)

    @pl.when(k5 < OFFS)
    def _():
        vis_block(5, k5)

    part_copy.wait_recv()
    beam[...] += in_part[...].astype(F32)
    cut = LT - 1
    late = (s + 2) % NS
    arrive(2, *range(cut))
    acc[...] = products(blocks.at[2], left, 0, cut)
    head = beam[:, : cut * 128] + beam_part(blocks.at[2], wts, (0,), late, 0, cut)
    sums[...] = window_powers(head, lens, 0)
    arrive(2, cut)
    rest = beam[:, cut * 128 :] + beam_part(blocks.at[2], wts, (0,), late, cut, LT)
    total = sums[...] + window_powers(rest, lens, cut)
    for j in range(INTEG):
        power[j] = total[j : j + 1] / jnp.full((1, SHARE), lens[j], jnp.int32).astype(F32)

    def put(j, p, value):
        vis[0, 2, j, 0, p] = value

    average(acc[...] + products(blocks.at[2], left, cut, LT), lens, put)
    for cp in sends:
        cp.wait_send()
    for q in range(NCH):
        if q == 2:
            pl.when(y < 3)(copy(0, 2, q, UP).wait_send)
        else:
            copy(0, 2, q, UP).wait_send()
    pl.when(y == 1)(spare_copy.wait_send)
    pl.when(y < 2)(copy(1, 5, NCH - 1, ACROSS).wait_send)
    pl.when(middle)(fifth_copy.wait_send)
    part_copy.wait_send()


def store_kernel(vis_in, power_in, vis, power, sem):
    copies = [
        pltpu.make_async_copy(vis_in, vis, sem.at[0]),
        pltpu.make_async_copy(power_in, power, sem.at[1]),
    ]
    for cp in copies:
        cp.start()
    for cp in copies:
        cp.wait()


def store(vis, power):
    return pl.pallas_call(
        store_kernel,
        out_shape=(
            jax.ShapeDtypeStruct(vis.shape, vis.dtype),
            jax.ShapeDtypeStruct(power.shape, power.dtype),
        ),
        in_specs=[pl.BlockSpec(memory_space=pl.ANY)] * 2,
        out_specs=(pl.BlockSpec(memory_space=pltpu.HBM), pl.BlockSpec(memory_space=pltpu.HBM)),
        scratch_shapes=[pltpu.SemaphoreType.DMA((2,))],
        compiler_params=pltpu.CompilerParams(vmem_limit_bytes=VMEM_LIMIT),
        name="store",
    )(vis, power)


def local(voltages, phase_index, int_lengths, beam_weights):
    vis, power = pl.pallas_call(
        kernel,
        out_shape=(
            jax.ShapeDtypeStruct((1, OFFS, INTEG, 1, 2, BLK, BLK), BF),
            jax.ShapeDtypeStruct((INTEG, 1, SHARE), F32),
        ),
        in_specs=[
            pl.BlockSpec(memory_space=pltpu.HBM),
            pl.BlockSpec(memory_space=pltpu.HBM),
            pl.BlockSpec(memory_space=pltpu.HBM),
            pl.BlockSpec(memory_space=pltpu.HBM),
        ],
        out_specs=(pl.BlockSpec(memory_space=pltpu.VMEM), pl.BlockSpec(memory_space=pltpu.VMEM)),
        scratch_shapes=[
            pltpu.SMEM((INTEG,), jnp.int32),
            pltpu.SMEM((INTEG,), jnp.int32),
            pltpu.VMEM((NS, 2, LT, NC, 4, 128), BF),
            pltpu.VMEM((NC, 2, 4, SAMPLES), BF),
            pltpu.VMEM((LT, NC, 2, 4, 128), BF),
            pltpu.VMEM((NC, 8, 128), F32),
            pltpu.VMEM((2, 2, SHARE, NS * BLK), BF),
            pltpu.VMEM((INTEG * BLK, 2 * SAMPLES), BF),
            pltpu.VMEM((2 * SHARE, SAMPLES), F32),
            pltpu.VMEM((INTEG * BLK, 2 * BLK), F32),
            pltpu.VMEM((8, SHARE), F32),
            pltpu.VMEM((ROWS, SAMPLES), BF),
            pltpu.VMEM((ROWS, SAMPLES), BF),
            pltpu.SemaphoreType.DMA((5,)),
            pltpu.SemaphoreType.DMA((NCH,)),
            pltpu.SemaphoreType.DMA((NCH,)),
            pltpu.SemaphoreType.DMA((NCH,)),
            pltpu.SemaphoreType.DMA((NS, NCH)),
            pltpu.SemaphoreType.DMA((NS, NCH)),
            pltpu.SemaphoreType.DMA,
            pltpu.SemaphoreType.DMA,
        ],
        compiler_params=pltpu.CompilerParams(
            collective_id=0, has_side_effects=True, vmem_limit_bytes=VMEM_LIMIT
        ),
        name="correlator",
    )(
        *[
            pltpu.with_memory_space_constraint(x, pltpu.HBM)
            for x in (phase_index, int_lengths, voltages, beam_weights)
        ]
    )
    return store(vis, power)


def solution(mesh):
    return jax.shard_map(
        local,
        mesh=mesh,
        in_specs=(P(None, None, ("stn", "chan"), None), P(("stn", "chan")), P(), P()),
        out_specs=(P("stn", None, None, "chan", None, None, None), P(None, "chan", "stn")),
        check_vma=False,
    )
```

```python
import functools
import math

import jax
import jax.numpy as jnp
from jax import lax
from jax.experimental import pallas as pl
from jax.experimental.pallas import tpu as pltpu
from jax.sharding import PartitionSpec as P

INTEG = 4
BEAMS = 256
PHASES = 1024
NC = 32
NS = 8
LT = 4
SAMPLES = 512
BLK = 128
OFFS = 5
SHARE = BEAMS // NS
NCH = LT
BF = jnp.bfloat16
FAR = sorted(range(1, NC), key=lambda k: -min(k % 16, 16 - k % 16))
F32 = jnp.float32
VMEM_LIMIT = 24 * 2**20
MESH = pl.DeviceIdType.MESH


def rotate_all(ph, vin, sbuf, trig):
    row = lax.broadcasted_iota(jnp.int32, (NC, 8, 128), 1)
    chan = lax.broadcasted_iota(jnp.int32, (NC, 8, 128), 0)
    col = row % 4
    step = jnp.where(col == 0, ph[0], jnp.where(col == 1, ph[1], jnp.where(col == 2, ph[2], ph[3])))
    turns = chan * step - jnp.where(row >= 4, PHASES // 4, 0)
    turns = ((turns + PHASES // 2) & (PHASES - 1)) - PHASES // 2
    trig[...] = jnp.cos(turns.astype(F32) * (2.0 * math.pi / PHASES))

    def one(c, carry):
        cs = trig[c]
        cos, sin = cs[0:4], cs[4:8]
        re = vin[c, 0].astype(F32)
        im = vin[c, 1].astype(F32)
        for t in range(LT):
            a = re[:, t * 128 : (t + 1) * 128]
            b = im[:, t * 128 : (t + 1) * 128]
            sbuf[t, c, 0] = (a * cos + b * sin).astype(BF)
            sbuf[t, c, 1] = (b * cos - a * sin).astype(BF)
        return carry

    lax.fori_loop(0, NC, one, 0, unroll=4)


def window_edges(lens):
    edges = [jnp.int32(0)]
    for j in range(INTEG):
        edges.append(edges[-1] + lens[j])
    return edges


def build_windows(blk, lens, left):
    edges = window_edges(lens)
    lane = lax.broadcasted_iota(jnp.int32, (1, 128), 1)
    for t in range(LT):
        at = lane + t * 128
        for j in range(INTEG):
            keep = ((at >= edges[j]) & (at < edges[j + 1])).astype(F32).astype(BF)
            for p in range(2):
                left[j * BLK : (j + 1) * BLK, (p * LT + t) * 128 : (p * LT + t + 1) * 128] = (
                    blk[p, t] * keep
                )


def products(blk, left, lo, hi):
    re = [blk[0, t] for t in range(lo, hi)]
    im = [blk[1, t] for t in range(lo, hi)]
    neg = [-x for x in im]
    right = jnp.concatenate(
        [jnp.concatenate(re + im, axis=1), jnp.concatenate(neg + re, axis=1)], axis=0
    )
    if (lo, hi) == (0, LT):
        rows = left[...]
    else:
        rows = jnp.concatenate(
            [left[:, (p * LT + lo) * 128 : (p * LT + hi) * 128] for p in range(2)], axis=1
        )
    return lax.dot_general(rows, right, (((1,), (1,)), ((), ())), preferred_element_type=F32)


def average(prod, lens, put):
    for j in range(INTEG):
        inverse = 1.0 / jnp.full((1, 128), lens[j], jnp.int32).astype(F32)
        for p in range(2):
            put(j, p, (prod[j * BLK : (j + 1) * BLK, p * 128 : (p + 1) * 128] * inverse).astype(BF))


def beam_part(blk, wts, dests, q, lo, hi):
    cols = pl.ds(pl.multiple_of(q * BLK, BLK), BLK)
    rows = []
    for d in dests:
        wr = wts[d, 0, :, cols]
        wi = wts[d, 1, :, cols]
        rows.append(jnp.concatenate([wr, -wi], axis=1))
        rows.append(jnp.concatenate([wi, wr], axis=1))
    stack = jnp.concatenate(rows, axis=0)
    parts = []
    for t in range(lo, hi, 2):
        x = jnp.concatenate(
            [jnp.concatenate([blk[p, u] for u in range(t, min(t + 2, hi))], axis=1) for p in range(2)],
            axis=0,
        )
        parts.append(jnp.dot(stack, x, preferred_element_type=F32))
    return jnp.concatenate(parts, axis=1)


def window_powers(beam, lens, lo):
    power = beam[:SHARE] ** 2 + beam[SHARE:] ** 2
    width = beam.shape[1]
    edges = window_edges(lens)
    at = lax.broadcasted_iota(jnp.int32, (8, width), 1) + lo * 128
    row = lax.broadcasted_iota(jnp.int32, (8, width), 0)
    mask = jnp.zeros((8, width), F32)
    for j in range(INTEG):
        inside = (row == j) & (at >= edges[j]) & (at < edges[j + 1])
        mask = jnp.where(inside, 1.0, mask)
    return lax.dot_general(
        mask, power, (((1,), (1,)), ((), ())), precision=lax.Precision.HIGHEST,
        preferred_element_type=F32,
    )


UP, DOWN, ACROSS = (0, 1), (0, -1), (1, 0)
FIRST = ((0, 1, UP), (0, 3, DOWN), (0, 4, ACROSS))
ROWS = 2 * SHARE


def kernel(
    ph_hbm, lens_hbm, v_hbm, w_hbm, vis, power,
    ph, lens, g, vin, sbuf, trig, wts, left, beam, acc, sums, out_part, in_part, lsem, o1, s1, r1, s2, r2, s3, r3,
):
    c = lax.axis_index("chan")
    s = lax.axis_index("stn")
    h, y = s // 4, s % 4

    def to(step):
        return {"chan": c, "stn": ((h + step[0]) % 2) * 4 + (y + step[1] + 4) % 4}

    barrier = pltpu.get_barrier_semaphore()

    for step in (UP, DOWN, ACROSS):
        pl.semaphore_signal(barrier, 1, device_id=to(step), device_id_type=MESH)
    for k in (2, NS - 2):
        pl.semaphore_signal(
            barrier, 1, device_id={"chan": c, "stn": (s + k) % NS}, device_id_type=MESH
        )
    for k in FAR:
        pl.semaphore_signal(
            barrier, 1, device_id={"chan": (c + k) % NC, "stn": s}, device_id_type=MESH
        )
    load = pltpu.make_async_copy(v_hbm, vin, lsem.at[0])
    load.start()
    load_p = pltpu.make_async_copy(ph_hbm, ph, lsem.at[3])
    load_p.start()
    load_l = pltpu.make_async_copy(lens_hbm, lens, lsem.at[4])
    load_l.start()
    load_w = [
        pltpu.make_async_copy(
            w_hbm.at[:, pl.ds(pl.multiple_of(d * SHARE, SHARE), SHARE)], wts.at[i], lsem.at[i + 1]
        )
        for i, d in enumerate((s, (s + 2) % NS))
    ]
    for cp in load_w:
        cp.start()
    load_p.wait()
    load.wait()
    rotate_all(ph, vin, sbuf, trig)
    pl.semaphore_wait(barrier, NC - 1 + 5)

    for q in range(NCH):
        for k in FAR:
            d = (c + k) % NC
            pltpu.make_async_remote_copy(
                sbuf.at[q, d], g.at[0, :, q, c], s1.at[q], r1.at[q],
                device_id={"chan": d, "stn": s}, device_id_type=MESH,
            ).start()
    owns = [
        pltpu.make_async_copy(sbuf.at[q, c], g.at[0, :, q, c], o1.at[q]) for q in range(NCH)
    ]
    for cp in owns:
        cp.start()
    for cp in owns:
        cp.wait()
    for cp in load_w:
        cp.wait()
    load_l.wait()

    sends = []
    have = {(0, q) for q in range(NCH)}

    def copy(src, dst, q, step):
        return pltpu.make_async_remote_copy(
            g.at[src, :, q], g.at[dst, :, q], s2.at[dst, q], r2.at[dst, q],
            device_id=to(step), device_id_type=MESH,
        )

    def arrive(slot, *chunks):
        for q in chunks:
            if (slot, q) not in have:
                copy(0, slot, q, UP).wait_recv()
                have.add((slot, q))

    def push(src, dst, step, q):
        arrive(src, q)
        cp = copy(src, dst, q, step)
        cp.start()
        sends.append(cp)

    blocks = g.reshape(NS, 2, LT, BLK, 128)

    def block_at(slot):
        dh, dy = slot // 4, slot % 4
        q = ((h + dh) % 2) * 4 + (y - dy + 4) % 4
        return q, (q - s + NS) % NS

    def process(slot):
        arrive(slot, *range(NCH))
        q, k = block_at(slot)
        part = beam_part(blocks.at[slot], wts, (0,), q, 0, LT)
        beam[...] += part

        @pl.when(k < OFFS)
        def _():
            vis_block(slot, k)

    def vis_block(slot, k):
        def put(j, p, value):
            vis[0, k, j, 0, p] = value

        average(products(blocks.at[slot], left, 0, LT), lens, put)

    middle = (y == 1) | (y == 2)
    part_copy = pltpu.make_async_remote_copy(
        out_part, in_part, s3, r3,
        device_id={"chan": c, "stn": (s + 2) % NS}, device_id_type=MESH,
    )

    fifth_copy = pltpu.make_async_remote_copy(
        g.at[4, :, NCH - 1], g.at[5, :, NCH - 1], s2.at[6, 1], r2.at[5, NCH - 1],
        device_id=to(UP), device_id_type=MESH,
    )
    spare_copy = pltpu.make_async_remote_copy(
        g.at[3, :, 2], g.at[2, :, 2], s2.at[6, 0], r2.at[2, 2],
        device_id=to(DOWN), device_id_type=MESH,
    )

    for q in range(NCH):
        turned = pltpu.make_async_remote_copy(
            sbuf.at[q, pl.ds(0, NC - 1)], g.at[0, :, q, pl.ds(0, NC - 1)], s1.at[q], r1.at[q],
            device_id=to(UP), device_id_type=MESH,
        )
        turned.wait_recv()
        for src, dst, step in FIRST:
            push(src, dst, step, q)
        turned.wait_send()
    part = beam_part(blocks.at[0], wts, (0, 1), s, 0, LT)
    beam[...] = part[:ROWS]
    out_part[...] = part[ROWS:].astype(BF)
    build_windows(blocks.at[0], lens, left)
    vis_block(0, 0)
    part_copy.start()
    for q in range(NCH):
        if q % 2 == 0:
            push(3, 7, ACROSS, q)
            push(4, 5, UP, q)
        else:
            if q < NCH - 1:
                push(1, 5, ACROSS, q)
            else:
                arrive(1, q)
                pl.when(y < 2)(copy(1, 5, q, ACROSS).start)
            push(4, 7, DOWN, q)
            if q == NCH - 1:
                pl.when(middle)(fifth_copy.start)
    for q in range(NCH):
        arrive(1 if q % 2 == 0 else 3, q)

        sender = (y == 0) if q == 2 else ~middle if q % 2 == 0 else middle

        @pl.when(sender)
        def _():
            if q % 2 == 0:
                copy(1, 2, q, UP).start()
            else:
                copy(3, 2, q, DOWN).start()

        if q == 2:
            arrive(3, q)
            pl.when(y == 1)(spare_copy.start)

    def last_hop(q):
        if q % 2 == 0:
            arrive(5, q)

            @pl.when(middle)
            def _():
                copy(5, 2, q, UP).start()
        else:
            arrive(7, q)

            @pl.when(~middle)
            def _():
                copy(7, 2, q, DOWN).start()

    process(4)
    process(1)
    last_hop(0)
    last_hop(1)
    process(3)
    last_hop(2)
    last_hop(3)
    process(7)
    q5, k5 = block_at(5)
    arrive(5, 0, 1, 2)
    beam[:, : 3 * 128] += beam_part(blocks.at[5], wts, (0,), q5, 0, 3)
    arrive(5, 3)
    beam[:, 3 * 128 :] += beam_part(blocks.at[5], wts, (0,), q5, 3, LT)

    @pl.when(k5 < OFFS)
    def _():
        vis_block(5, k5)

    part_copy.wait_recv()
    beam[...] += in_part[...].astype(F32)
    cut = LT - 1
    late = (s + 2) % NS
    arrive(2, *range(cut))
    acc[...] = products(blocks.at[2], left, 0, cut)
    head = beam[:, : cut * 128] + beam_part(blocks.at[2], wts, (0,), late, 0, cut)
    sums[...] = window_powers(head, lens, 0)
    arrive(2, cut)
    rest = beam[:, cut * 128 :] + beam_part(blocks.at[2], wts, (0,), late, cut, LT)
    total = sums[...] + window_powers(rest, lens, cut)
    for j in range(INTEG):
        power[j] = total[j : j + 1] / jnp.full((1, SHARE), lens[j], jnp.int32).astype(F32)

    def put(j, p, value):
        vis[0, 2, j, 0, p] = value

    average(acc[...] + products(blocks.at[2], left, cut, LT), lens, put)
    for cp in sends:
        cp.wait_send()
    for q in range(NCH):
        if q == 2:
            pl.when(y < 3)(copy(0, 2, q, UP).wait_send)
        else:
            copy(0, 2, q, UP).wait_send()
    pl.when(y == 1)(spare_copy.wait_send)
    pl.when(y < 2)(copy(1, 5, NCH - 1, ACROSS).wait_send)
    pl.when(middle)(fifth_copy.wait_send)
    part_copy.wait_send()


def store_kernel(vis_in, power_in, vis, power, sem):
    copies = [
        pltpu.make_async_copy(vis_in, vis, sem.at[0]),
        pltpu.make_async_copy(power_in, power, sem.at[1]),
    ]
    for cp in copies:
        cp.start()
    for cp in copies:
        cp.wait()


def store(vis, power):
    return pl.pallas_call(
        store_kernel,
        out_shape=(
            jax.ShapeDtypeStruct(vis.shape, vis.dtype),
            jax.ShapeDtypeStruct(power.shape, power.dtype),
        ),
        in_specs=[pl.BlockSpec(memory_space=pl.ANY)] * 2,
        out_specs=(pl.BlockSpec(memory_space=pltpu.HBM), pl.BlockSpec(memory_space=pltpu.HBM)),
        scratch_shapes=[pltpu.SemaphoreType.DMA((2,))],
        compiler_params=pltpu.CompilerParams(vmem_limit_bytes=VMEM_LIMIT),
        name="store",
    )(vis, power)


def local(voltages, phase_index, int_lengths, beam_weights):
    vis, power = pl.pallas_call(
        kernel,
        out_shape=(
            jax.ShapeDtypeStruct((1, OFFS, INTEG, 1, 2, BLK, BLK), BF),
            jax.ShapeDtypeStruct((INTEG, 1, SHARE), F32),
        ),
        in_specs=[
            pl.BlockSpec(memory_space=pltpu.HBM),
            pl.BlockSpec(memory_space=pltpu.HBM),
            pl.BlockSpec(memory_space=pltpu.HBM),
            pl.BlockSpec(memory_space=pltpu.HBM),
        ],
        out_specs=(pl.BlockSpec(memory_space=pltpu.VMEM), pl.BlockSpec(memory_space=pltpu.VMEM)),
        scratch_shapes=[
            pltpu.SMEM((INTEG,), jnp.int32),
            pltpu.SMEM((INTEG,), jnp.int32),
            pltpu.VMEM((NS, 2, LT, NC, 4, 128), BF),
            pltpu.VMEM((NC, 2, 4, SAMPLES), BF),
            pltpu.VMEM((LT, NC, 2, 4, 128), BF),
            pltpu.VMEM((NC, 8, 128), F32),
            pltpu.VMEM((2, 2, SHARE, NS * BLK), BF),
            pltpu.VMEM((INTEG * BLK, 2 * SAMPLES), BF),
            pltpu.VMEM((2 * SHARE, SAMPLES), F32),
            pltpu.VMEM((INTEG * BLK, 2 * BLK), F32),
            pltpu.VMEM((8, SHARE), F32),
            pltpu.VMEM((ROWS, SAMPLES), BF),
            pltpu.VMEM((ROWS, SAMPLES), BF),
            pltpu.SemaphoreType.DMA((5,)),
            pltpu.SemaphoreType.DMA((NCH,)),
            pltpu.SemaphoreType.DMA((NCH,)),
            pltpu.SemaphoreType.DMA((NCH,)),
            pltpu.SemaphoreType.DMA((NS, NCH)),
            pltpu.SemaphoreType.DMA((NS, NCH)),
            pltpu.SemaphoreType.DMA,
            pltpu.SemaphoreType.DMA,
        ],
        compiler_params=pltpu.CompilerParams(
            collective_id=0, has_side_effects=True, vmem_limit_bytes=VMEM_LIMIT
        ),
        name="correlator",
    )(
        *[
            pltpu.with_memory_space_constraint(x, pltpu.HBM)
            for x in (phase_index, int_lengths, voltages, beam_weights)
        ]
    )
    return store(vis, power)


def solution(mesh):
    return jax.shard_map(
        local,
        mesh=mesh,
        in_specs=(P(None, None, ("stn", "chan"), None), P(("stn", "chan")), P(), P()),
        out_specs=(P("stn", None, None, "chan", None, None, None), P(None, "chan", "stn")),
        check_vma=False,
    )
```
